256 devices in a mesh: grp: 16 (over x, y), tile: 16 (over z, core).
Axes of the slice: x: 4, y: 4, z: 8, core: 2. Of those that a mesh axis runs over, the one named last changes fastest.
Arguments:
- starting_realizations: float32 [1024, 2, 4, 128, 128], P('grp', None, None, 'tile'), may hold values from -6 to 6
- diffusivity: float32 [4, 128], replicated, may hold values from 0.1 to 0.24
- eastward_velocity: float32 [4], replicated, may hold values from -0.4 to 0.4
- northward_velocity: float32 [4], replicated, may hold values from -0.4 to 0.4
- obs_cell: int32 [16, 16, 256], P('tile'), may hold values from 0 to 2047
- obs_count: int32 [16, 16], P('tile', 'grp'), may hold values from 1 to 256
- obs_value: float32 [16, 16, 256], P('tile', 'grp'), may hold values from -15 to 15
- obs_weight: float32 [16, 16, 256], P('tile', 'grp'), may hold values from 0.05 to 0.5
Outputs:
- analysis: bfloat16 [1024, 2, 4, 128, 128], P('grp', None, None, 'tile')
The draws below stay inside these ranges and needn't reach their ends.
All inputs are finite; a program needn't handle non-finite values.
Results may differ from the reference program's by a relative error of at most 0.0062.
Values may be sent and summed in bfloat16 or wider, within the bound.
A program may use at most 128 MiB of HBM per device.

```python
import math
import jax
import jax.numpy as jnp
from jax import lax

REALIZATIONS = 1024
LAYER_NUMBER = 4
TILE_SPAN = 8
STEPS = 2
OBS = 256
GRID_SPAN_FIRST = 128
GRID_SPAN_SECOND = 128
STATE = 512
REGION = 2048
N_GRP = 16
N_TILE = 16


def touch_ends(values, own_key, least, top_value):
    extent = values.shape
    place = [jax.random.randint(jax.random.fold_in(own_key, axis), (), 0, extent[axis]) for axis in range(len(extent))]
    values = values.at[tuple(place)].set(least)
    longest = extent.index(max(extent))
    place[longest] = (place[longest] + 1) % extent[longest]
    return values.at[tuple(place)].set(top_value)


def block_levels(own_key, dims, pieces, least, largest):
    def one(position, blocks):
        heights = jax.random.uniform(jax.random.fold_in(jax.random.fold_in(own_key, 6), position), (blocks,), jnp.float32, least / len(pieces), largest / len(pieces))
        return jnp.repeat(jnp.exp(heights), dims[position] // blocks).reshape((-1,) + (1,) * (len(dims) - position - 1))

    factor_of = one(*pieces[0])
    for cut in pieces[1:]:
        factor_of = factor_of * one(*cut)
    return factor_of


def gaussian(rng, dims, width, bound, shards=(), kind=jnp.bfloat16):
    entries = width * jax.random.normal(rng, dims, jnp.float32)
    if shards:
        entries = entries * block_levels(rng, dims, shards, -0.22, 0.18)
    return jnp.clip(entries, -bound, bound).astype(kind)


def setup_inputs(seed: int = 0) -> dict:
    arg_keys = jax.random.split(jax.random.key(seed), 9)
    starting_realizations = gaussian(arg_keys[0], (REALIZATIONS, 2, LAYER_NUMBER, GRID_SPAN_FIRST, GRID_SPAN_SECOND), 1.0, 6.0, ((0, 16), (3, 16)), jnp.float32)
    diffusivity = jnp.clip(jnp.exp(jax.random.uniform(arg_keys[1], (LAYER_NUMBER, GRID_SPAN_SECOND), jnp.float32, math.log(0.1), math.log(0.24))), 0.1, 0.24)
    eastward_velocity = jnp.clip(jax.random.uniform(arg_keys[2], (LAYER_NUMBER,), jnp.float32, -0.4, 0.4), -0.4, 0.4)
    northward_velocity = jnp.clip(jax.random.uniform(arg_keys[3], (LAYER_NUMBER,), jnp.float32, -0.4, 0.4), -0.4, 0.4)
    obs_cell = touch_ends(jax.random.randint(arg_keys[4], (N_TILE, N_GRP, OBS), 0, REGION), jax.random.fold_in(arg_keys[4], 1), 0, REGION - 1).astype(jnp.int32)
    obs_count = touch_ends(jax.random.randint(arg_keys[5], (N_TILE, N_GRP), 1, OBS + 1), jax.random.fold_in(arg_keys[5], 1), 1, OBS).astype(jnp.int32)
    obs_value = gaussian(arg_keys[6], (N_TILE, N_GRP, OBS), 3.0, 15.0, ((0, 16), (1, 16)), jnp.float32)
    obs_weight = jnp.clip(jnp.exp(math.log(0.5) - 2.3025851 * jax.random.uniform(arg_keys[7], (N_TILE, N_GRP, OBS), jnp.float32) ** block_levels(arg_keys[7], (N_TILE, N_GRP, OBS), ((0, 16), (1, 16)), -0.2, 0.2)), 0.05, 0.5)
    return {"starting_realizations": starting_realizations, "diffusivity": diffusivity, "eastward_velocity": eastward_velocity, "northward_velocity": northward_velocity, "obs_cell": obs_cell, "obs_count": obs_count, "obs_value": obs_value, "obs_weight": obs_weight}


HIGH = lax.Precision.HIGHEST

def tendency(center, east_cell, west_cell, north_cell, south_cell, diffusivity, eastward_velocity, northward_velocity):
    laplace = east_cell + west_cell + north_cell + south_cell - 4.0 * center
    transport = eastward_velocity[:, None, None] * (east_cell - west_cell) * 0.5 + northward_velocity[:, None, None] * (north_cell - south_cell) * 0.5
    return center + diffusivity[:, None, :] * laplace - transport

def analyze(packed):
    realization_fields, measured_realizations, obs_total, obs_value, obs_weight = packed
    members = realization_fields.shape[0]
    average = lax.optimization_barrier(jnp.mean(measured_realizations, 0))
    obs_dev = measured_realizations - average
    active = (jnp.arange(OBS) < obs_total).astype(jnp.float32)
    obs_scale = active * obs_weight
    weighted = obs_dev * obs_scale
    gram_sum = jnp.dot(weighted, obs_dev.T, precision=HIGH, preferred_element_type=jnp.float32)
    innovation = jnp.dot(weighted, obs_value - average, precision=HIGH, preferred_element_type=jnp.float32)
    identity = jnp.eye(members, dtype=jnp.float32)
    system = gram_sum + (members - 1.0) * identity
    trace_mean = jnp.trace(system) / members
    first_iter = system / trace_mean
    first_poly = 1.5 * identity - 0.5 * first_iter
    second_iter = jnp.dot(first_iter, first_poly, precision=HIGH, preferred_element_type=jnp.float32)
    second_poly = 1.5 * identity - 0.5 * jnp.dot(first_poly, second_iter, precision=HIGH, preferred_element_type=jnp.float32)
    root_iter = jnp.dot(second_poly, first_poly, precision=HIGH, preferred_element_type=jnp.float32)
    inv_root = root_iter / jnp.sqrt(trace_mean)
    mean_weights = jnp.dot(inv_root, jnp.dot(inv_root, innovation, precision=HIGH, preferred_element_type=jnp.float32), precision=HIGH, preferred_element_type=jnp.float32)
    weights = (jnp.sqrt(members - 1.0) * inv_root + mean_weights[:, None]).astype(jnp.bfloat16)
    flat_states = realization_fields.astype(jnp.float32)
    centre = lax.optimization_barrier(jnp.mean(flat_states, 0))
    deviation = (flat_states - centre).astype(jnp.bfloat16)
    updated = centre + lax.dot_general(weights, deviation, (((0,), (0,)), ((), ())), preferred_element_type=jnp.float32)
    return updated.astype(jnp.bfloat16)

def reference(starting_realizations, diffusivity, eastward_velocity, northward_velocity, obs_cell, obs_count, obs_value, obs_weight):

    def handle_bundle(member_batch):
        field_now = member_batch
        for repeat in range(STEPS):
            field_now = tendency(field_now, jnp.roll(field_now, -1, 3), jnp.roll(field_now, 1, 3), jnp.roll(field_now, -1, 4), jnp.roll(field_now, 1, 4), diffusivity, eastward_velocity, northward_velocity)
        return field_now
    bundled_subdomains = starting_realizations.reshape(N_GRP, REALIZATIONS // N_GRP, 2, LAYER_NUMBER, GRID_SPAN_FIRST, GRID_SPAN_SECOND)
    predicted_field = lax.map(handle_bundle, bundled_subdomains).reshape(REALIZATIONS, 2, LAYER_NUMBER, GRID_SPAN_FIRST, GRID_SPAN_SECOND)
    tile_index = jnp.arange(N_TILE, dtype=jnp.int32)[:, None, None]
    block_index = jnp.arange(N_GRP, dtype=jnp.int32)[None, :, None]
    layer_index = obs_cell // (4 * TILE_SPAN * TILE_SPAN)
    remainder = obs_cell % (4 * TILE_SPAN * TILE_SPAN)
    row_off = remainder // (2 * TILE_SPAN)
    col_off = remainder % (2 * TILE_SPAN)
    row_global = (tile_index * TILE_SPAN - TILE_SPAN // 2 + row_off) % GRID_SPAN_FIRST
    col_global = (block_index * TILE_SPAN - TILE_SPAN // 2 + col_off) % GRID_SPAN_SECOND
    flattened_position = ((layer_index * GRID_SPAN_FIRST + row_global) * GRID_SPAN_SECOND + col_global).astype(jnp.int32)
    measured_realizations = jnp.take(predicted_field.reshape(REALIZATIONS, -1), flattened_position.reshape(-1), axis=1)
    measured_realizations = measured_realizations.reshape(REALIZATIONS, N_TILE * N_GRP, OBS).transpose(1, 0, 2)
    realization_fields = predicted_field.astype(jnp.bfloat16).reshape(REALIZATIONS, 2, LAYER_NUMBER, N_TILE, TILE_SPAN, N_GRP, TILE_SPAN)
    realization_fields = realization_fields.transpose(3, 5, 0, 1, 2, 4, 6).reshape(N_TILE * N_GRP, REALIZATIONS, STATE)
    result = lax.map(analyze, (realization_fields, measured_realizations, obs_count.reshape(-1), obs_value.reshape(-1, OBS), obs_weight.reshape(-1, OBS)))
    result = result.reshape(N_TILE, N_GRP, REALIZATIONS, 2, LAYER_NUMBER, TILE_SPAN, TILE_SPAN).transpose(2, 3, 4, 0, 5, 1, 6)
    return result.reshape(REALIZATIONS, 2, LAYER_NUMBER, GRID_SPAN_FIRST, GRID_SPAN_SECOND)
```

```python
import jax
import jax.numpy as jnp
from jax import lax
from jax.experimental import pallas as pl
from jax.experimental.pallas import tpu as pltpu
from jax.sharding import PartitionSpec as P


F32 = jnp.float32
BF16 = jnp.bfloat16
HIGH = lax.Precision.HIGHEST
VMEM = pl.BlockSpec(memory_space=pltpu.VMEM)
SMEM = pl.BlockSpec(memory_space=pltpu.SMEM)
MEMBERS = 1024.0
PARAMS = pltpu.CompilerParams(vmem_limit_bytes=48 * 1024 * 1024)


def nt(a, b, precision=None):
    return lax.dot_general(a, b, (((1,), (1,)), ((), ())), precision=precision, preferred_element_type=F32)


def nn(a, b, precision=None):
    return lax.dot_general(a, b, (((1,), (0,)), ((), ())), precision=precision, preferred_element_type=F32)


def turn_in(x_ref, z_ref, low_ref, high_ref):
    for row in range(8):
        for level in range(4):
            start = level * 8 + row
            plane = jnp.concatenate(
                [x_ref[pl.ds(start, 64, stride=64), :], x_ref[pl.ds(start + 32, 64, stride=64), :]], axis=0
            )
            z_ref[pl.ds((row // 2) * 1024 + (row % 2) * 4 + level, 128, stride=8), :] = plane.T
    low_ref[...] = z_ref[0:1024, :].astype(BF16)
    high_ref[...] = z_ref[3072:4096, :].astype(BF16)


def stencil(v_ref, k_list, y0, count, coef, sub):
    d, u, v = coef
    east_c, west_c, north_c, south_c = d - u, d + u, d - v, d + v
    mid_c = 1.0 - 4.0 * d
    upper = sub < 4
    centers = {}
    rolled = {}
    for k in range(6):
        centers[k] = v_ref[k, pl.ds(y0 + 1, count)]
        rolled[k] = pltpu.roll(centers[k], 4, 1)
    outs = []
    for k in k_list:
        east = jnp.where(upper, rolled[k], rolled[k + 1]) if k < 5 else rolled[k]
        west = jnp.where(upper, rolled[k - 1], rolled[k]) if k > 0 else rolled[k]
        north = v_ref[k, pl.ds(y0 + 2, count)]
        south = v_ref[k, pl.ds(y0, count)]
        outs.append(centers[k] * mid_c + east * east_c + west * west_c + north * north_c + south * south_c)
    return outs


def wrap(v_ref):
    for k in range(6):
        v_ref[k, 0] = v_ref[k, 128]
        v_ref[k, 129] = v_ref[k, 1]


def forecast(z_ref, low_ref, high_ref, d_ref, u_ref, v_ref, s_ref, down_ref, up_ref, first, second):
    first[0, 1:129] = low_ref[...].astype(F32).reshape(128, 8, 128)
    first[5, 1:129] = high_ref[...].astype(F32).reshape(128, 8, 128)
    for k in range(4):
        first[k + 1, 1:129] = z_ref[k * 1024:(k + 1) * 1024, :].reshape(128, 8, 128)
    wrap(first)
    sub = lax.broadcasted_iota(jnp.int32, (8, 8, 128), 1)
    u = 0.5 * u_ref[...][None]
    v = 0.5 * v_ref[...][None]

    @pl.loop(0, 16)
    def _(step):
        y0 = step * 8
        coef = (d_ref[pl.ds(y0, 8)], u, v)
        for k, value in enumerate(stencil(first, range(6), y0, 8, coef, sub)):
            second[k, pl.ds(y0 + 1, 8)] = value

    wrap(second)

    @pl.loop(0, 16)
    def _(step):
        y0 = step * 8
        coef = (d_ref[pl.ds(y0, 8)], u, v)
        for k, value in enumerate(stencil(second, range(1, 5), y0, 8, coef, sub)):
            packed = value.reshape(64, 128).astype(BF16)
            s_ref[step, k * 64:(k + 1) * 64, :] = packed
            if k < 2:
                down_ref[step, k * 64:(k + 1) * 64, :] = packed
            else:
                up_ref[step, (k - 2) * 64:(k - 1) * 64, :] = packed


def observe(s_ref, low_ref, high_ref, cell_ref, ob_ref):
    cell = cell_ref[...]
    level_index = cell // 256
    rest = cell % 256
    row = rest // 16
    col = rest % 16
    half = (level_index // 4)
    index = (row // 2) * 128 + col * 8 + (row % 2) * 4 + level_index % 4
    lane = lax.broadcasted_iota(jnp.int32, (256, 128), 1)
    left = lane < 64
    left_half = left[0:128]
    for b in range(16):
        before, after = (b + 15) % 16, (b + 1) % 16
        index_b = index[:, b:b + 1]
        half_b = half[:, b:b + 1]
        picks, pieces = [], []
        for kk in range(8):
            picks.append(jnp.where(index_b == lane + kk * 128, 1.0, 0.0).astype(BF16))
            if kk < 2:
                source, k = low_ref, kk
            elif kk < 6:
                source, k = s_ref, kk - 2
            else:
                source, k = high_ref, kk - 6
            pieces.append(source[before, k * 64 + 32:k * 64 + 64, :])
            pieces.append(source[b, k * 64:k * 64 + 64, :])
            pieces.append(source[after, k * 64:k * 64 + 32, :])
        values = nn(jnp.concatenate(picks, axis=1), jnp.concatenate(pieces, axis=0))
        values = jnp.where((half_b == 0) == left, values, 0.0)
        values = values + pltpu.roll(values, 64, 1)
        ob_ref[b] = jnp.where(left_half, values[0:128], values[128:256]).astype(BF16)


def solve(ob_ref, s_ref, weight_ref, value_ref, count_ref, out_ref, basis, dev_all):
    lane = lax.broadcasted_iota(jnp.int32, (128, 128), 1)
    left = lane < 64
    left2 = lax.broadcasted_iota(jnp.int32, (256, 128), 1) < 64
    total = ob_ref[0].astype(F32)
    for g in range(1, 16):
        total = total + ob_ref[g].astype(F32)
    mean0 = jnp.sum(jnp.where(left, total, 0.0), axis=1, keepdims=True) * (1.0 / MEMBERS)
    mean1 = jnp.sum(jnp.where(left, 0.0, total), axis=1, keepdims=True) * (1.0 / MEMBERS)
    count = count_ref[0, 0]
    row_lane = lax.broadcasted_iota(jnp.int32, (1, 128), 1)
    root0 = jnp.sqrt(jnp.where(row_lane < count, weight_ref[0:1, :], 0.0))
    root1 = jnp.sqrt(jnp.where(row_lane + 128 < count, weight_ref[1:2, :], 0.0))
    root0 = jnp.broadcast_to(root0, (128, 128)).T
    root1 = jnp.broadcast_to(root1, (128, 128)).T
    target0 = jnp.broadcast_to(value_ref[0:1, :], (128, 128)).T
    target1 = jnp.broadcast_to(value_ref[1:2, :], (128, 128)).T
    misfit = jnp.concatenate([root0 * (target0 - mean0), root1 * (target1 - mean1)], axis=0)
    mean = jnp.where(left, mean0, mean1)
    root = jnp.where(left, root0, root1)
    zero = jnp.zeros((256, 128), BF16)
    for g in range(16):
        scaled = (ob_ref[g].astype(F32) - mean) * root
        turned = pltpu.roll(scaled, 64, 1)
        both = jnp.concatenate(
            [jnp.where(left, scaled, turned), jnp.where(left, turned, scaled)], axis=0
        )
        basis[0:256, g * 128:(g + 1) * 128] = jnp.where(left2, both, 0.0).astype(BF16)
        basis[256:512, g * 128:(g + 1) * 128] = jnp.where(left2, 0.0, both).astype(BF16)
    small = nt(basis[0:256, :], basis[0:256, :])
    eye = lax.broadcasted_iota(jnp.int32, (256, 256), 0) == lax.broadcasted_iota(jnp.int32, (256, 256), 1)
    trace = jnp.sum(jnp.where(eye, small, 0.0), axis=(0, 1), keepdims=True)
    s = (MEMBERS - 1.0) + trace * (1.0 / MEMBERS)
    inv_s = 1.0 / s
    inv_root_s = lax.rsqrt(s)
    a = (MEMBERS - 1.0) * inv_s
    p = 1.5 - 0.5 * a
    r0 = 1.5 * p - 0.5 * a * p * p * p
    r1 = -0.75 - 0.5 * p * p * p + 0.75 * a * p * p
    r2 = 0.5 * (1.5 * p * p - 0.75 * a * p)
    r3 = (1.0 / 6.0) * (0.375 * a - 2.25 * p)
    r4 = 1.5 / 24.0
    g1 = small * inv_s
    g2 = nn(g1, g1, HIGH)
    q = jnp.where(eye, r1, 0.0) + r2 * g1 + r3 * g2 + r4 * nn(g2, g1, HIGH)
    first = (r0 * misfit + nn(g1, nn(q, misfit, HIGH), HIGH)) * inv_root_s
    gain = (r0 * first + nn(g1, nn(q, first, HIGH), HIGH)) * inv_root_s
    spread = jnp.sqrt(jnp.full((1, 1), MEMBERS - 1.0, F32))
    mix = q * (spread * inv_s * inv_root_s)
    keep = r0 * spread * inv_root_s

    state_total = s_ref[0].astype(F32)
    for g in range(1, 16):
        state_total = state_total + s_ref[g].astype(F32)
    centre0 = jnp.sum(jnp.where(left2, state_total, 0.0), axis=1, keepdims=True) * (1.0 / MEMBERS)
    centre1 = jnp.sum(jnp.where(left2, 0.0, state_total), axis=1, keepdims=True) * (1.0 / MEMBERS)
    centre = jnp.where(left2, centre0, centre1)
    for g in range(16):
        dev_all[:, g * 128:(g + 1) * 128] = (s_ref[g].astype(F32) - centre).astype(BF16)
    cross = nt(dev_all[...], basis[...])
    cross0, cross1 = cross[:, 0:256], cross[:, 256:512]
    update = jnp.concatenate([nn(cross0, mix, HIGH), nn(cross1, mix, HIGH)], axis=1).astype(BF16)
    offset = centre + jnp.where(left2, nn(cross0, gain, HIGH), nn(cross1, gain, HIGH))
    for g in range(16):
        lanes = slice(g * 128, (g + 1) * 128)
        out_ref[g] = (offset + keep * dev_all[:, lanes].astype(F32) + nn(update, basis[:, lanes])).astype(BF16)


def turn_out(r_ref, out_ref, field, stage):
    for b in range(16):
        for k in range(4):
            field[pl.ds(k * 1024 + b * 64, 64), :] = r_ref[b, k * 64:(k + 1) * 64, :].astype(F32)
    for row in range(8):
        for level in range(4):
            start = level * 8 + row
            plane = field[pl.ds((row // 2) * 1024 + (row % 2) * 4 + level, 128, stride=8), :].T
            stage[pl.ds(start, 64, stride=64), :] = plane[0:64]
            stage[pl.ds(start + 32, 64, stride=64), :] = plane[64:128]
    out_ref[...] = stage[...].astype(BF16)


def call_turn_in(x):
    return pl.pallas_call(
        turn_in,
        out_shape=(
            jax.ShapeDtypeStruct((4096, 128), F32),
            jax.ShapeDtypeStruct((1024, 128), BF16),
            jax.ShapeDtypeStruct((1024, 128), BF16),
        ),
        in_specs=[VMEM],
        out_specs=(VMEM, VMEM, VMEM),
        compiler_params=PARAMS,
        name="turn_in",
    )(x)


def call_forecast(z, low, high, d, u, v):
    return pl.pallas_call(
        forecast,
        out_shape=(
            jax.ShapeDtypeStruct((16, 256, 128), BF16),
            jax.ShapeDtypeStruct((16, 128, 128), BF16),
            jax.ShapeDtypeStruct((16, 128, 128), BF16),
        ),
        in_specs=[VMEM] * 6,
        out_specs=(VMEM, VMEM, VMEM),
        scratch_shapes=[pltpu.VMEM((6, 130, 8, 128), F32), pltpu.VMEM((6, 130, 8, 128), F32)],
        compiler_params=PARAMS,
        name="forecast",
    )(z, low, high, d, u, v)


def call_observe(s, low, high, cell):
    return pl.pallas_call(
        observe,
        out_shape=jax.ShapeDtypeStruct((16, 128, 128), BF16),
        in_specs=[VMEM] * 4,
        out_specs=VMEM,
        compiler_params=PARAMS,
        name="observe",
    )(s, low, high, cell)


def call_solve(ob, s, weight, value, count):
    return pl.pallas_call(
        solve,
        out_shape=jax.ShapeDtypeStruct((16, 256, 128), BF16),
        in_specs=[VMEM, VMEM, VMEM, VMEM, SMEM],
        out_specs=VMEM,
        scratch_shapes=[pltpu.VMEM((512, 2048), BF16), pltpu.VMEM((256, 2048), BF16)],
        compiler_params=PARAMS,
        name="solve",
    )(ob, s, weight, value, count)


def call_turn_out(r):
    return pl.pallas_call(
        turn_out,
        out_shape=jax.ShapeDtypeStruct((4096, 128), BF16),
        in_specs=[VMEM],
        out_specs=VMEM,
        scratch_shapes=[pltpu.VMEM((4096, 128), F32), pltpu.VMEM((4096, 128), F32)],
        compiler_params=PARAMS,
        name="turn_out",
    )(r)


def coefficients(diffusivity, eastward_velocity, northward_velocity):
    d = jnp.broadcast_to(jnp.concatenate([diffusivity, diffusivity], 0).T[:, :, None], (128, 8, 128))
    u = jnp.broadcast_to(jnp.concatenate([eastward_velocity] * 2)[:, None], (8, 128))
    v = jnp.broadcast_to(jnp.concatenate([northward_velocity] * 2)[:, None], (8, 128))
    return d, u, v


def exchange(values):
    return lax.all_to_all(values, "grp", split_axis=0, concat_axis=0, tiled=True)


def on_device(
    starting_realizations,
    diffusivity,
    eastward_velocity,
    northward_velocity,
    obs_cell,
    obs_count,
    obs_value,
    obs_weight,
):
    count = lax.axis_size("tile")
    forward = [(i, (i + 1) % count) for i in range(count)]
    backward = [((i + 1) % count, i) for i in range(count)]
    d, u, v = coefficients(diffusivity, eastward_velocity, northward_velocity)
    z, bottom, top = call_turn_in(starting_realizations.reshape(4096, 128))
    low = lax.ppermute(top, "tile", forward)
    high = lax.ppermute(bottom, "tile", backward)
    states, down, up = call_forecast(z, low, high, d, u, v)
    low = lax.ppermute(up, "tile", forward)
    high = lax.ppermute(down, "tile", backward)
    blocked = exchange(states)
    measured = exchange(call_observe(states, low, high, obs_cell[0].T))
    updated = call_solve(
        measured, blocked, obs_weight.reshape(2, 128), obs_value.reshape(2, 128), obs_count
    )
    return call_turn_out(exchange(updated)).reshape(64, 2, 4, 8, 128)


def solution(mesh):
    return jax.shard_map(
        on_device,
        mesh=mesh,
        in_specs=(
            P("grp", None, None, "tile", None),
            P(),
            P(),
            P(),
            P("tile", None, None),
            P("tile", "grp"),
            P("tile", "grp", None),
            P("tile", "grp", None),
        ),
        out_specs=P("grp", None, None, "tile", None),
        check_vma=False,
    )
```

```python
import jax
import jax.numpy as jnp
from jax import lax
from jax.experimental import pallas as pl
from jax.experimental.pallas import tpu as pltpu
from jax.sharding import PartitionSpec as P


F32 = jnp.float32
BF16 = jnp.bfloat16
HIGH = lax.Precision.HIGHEST
VMEM = pl.BlockSpec(memory_space=pltpu.VMEM)
SMEM = pl.BlockSpec(memory_space=pltpu.SMEM)
MEMBERS = 1024.0
MESH = pl.DeviceIdType.MESH
ANY = pl.BlockSpec(memory_space=pl.ANY)
PLACE = (2, 0, 1, 3)
PAIR = (1, 2, 0, 3)
SPAN = 130 * 8


def nt(a, b, precision=None):
    return lax.dot_general(a, b, (((1,), (1,)), ((), ())), precision=precision, preferred_element_type=F32)


def nn(a, b, precision=None):
    return lax.dot_general(a, b, (((1,), (0,)), ((), ())), precision=precision, preferred_element_type=F32)


def stencil(ref, k_list, low, high, y0, coef, upper):
    d, u, v = coef
    east_c, west_c, north_c, south_c = d - u, d + u, d - v, d + v
    mid_c = 1.0 - 4.0 * d

    def rows(k, shift):
        return ref[pl.ds(pl.multiple_of(k * SPAN + (y0 + 1 + shift) * 8, 8), 64), :].reshape(8, 8, 128)

    rolled = {}

    def roll(k):
        if k not in rolled:
            rolled[k] = pltpu.roll(rows(k, 0), 4, 1)
        return rolled[k]

    outs = []
    for k in k_list:
        east = jnp.where(upper, roll(k), roll(k + 1)) if k < high else roll(k)
        west = jnp.where(upper, roll(k - 1), roll(k)) if k > low else roll(k)
        outs.append(
            rows(k, 0) * mid_c + east * east_c + west * west_c + rows(k, 1) * north_c + rows(k, -1) * south_c
        )
    return outs


def wrap(ref, k_list):
    for k in k_list:
        ref[k * SPAN:k * SPAN + 8, :] = ref[k * SPAN + 1024:k * SPAN + 1032, :]
        ref[k * SPAN + 1032:k * SPAN + 1040, :] = ref[k * SPAN + 8:k * SPAN + 16, :]


def turn_in(x_ref, field, rows):
    for row in rows:
        for level in range(4):
            plane = jnp.concatenate(
                [x_ref[level, pl.ds(row, 64, stride=16), :], x_ref[level, pl.ds(8 + row, 64, stride=16), :]], axis=0
            )
            start = (row // 2 + 1) * SPAN + 8 + (row % 2) * 4 + level
            field[pl.ds(start, 128, stride=8), :] = plane.T


def forward(
    x_hbm, d_ref, u_ref, v_ref, cell_ref, ob_ref, dev_ref, centre_ref,
    x_ref, first, second, halo_out, halo_in, mine, blocked, region, seen, seen_out,
    load_sem, halo_send, halo_recv, state_send, state_recv, region_send, region_recv, ob_send, ob_recv,
):
    me = lax.axis_index("grp")
    tile = lax.axis_index("tile")
    tiles = lax.axis_size("tile")
    below, above = lax.rem(tile + tiles - 1, tiles), lax.rem(tile + 1, tiles)

    def other(i):
        return lax.rem(me + 1 + i, 16)

    loads = []
    for level in range(4):
        loads.append(pltpu.make_async_copy(x_hbm.at[:, level], x_ref.at[level].reshape(128, 8, 128), load_sem.at[level]))
        loads[-1].start()
    barrier = pltpu.get_barrier_semaphore()

    @pl.loop(0, 15)
    def _(i):
        pl.semaphore_signal(barrier, inc=1, device_id=(other(i), tile), device_id_type=MESH)

    pl.semaphore_signal(barrier, inc=1, device_id=(me, below), device_id_type=MESH)
    pl.semaphore_signal(barrier, inc=1, device_id=(me, above), device_id_type=MESH)

    def halo(side):
        return pltpu.make_async_remote_copy(
            src_ref=halo_out.at[side], dst_ref=halo_in.at[side], send_sem=halo_send.at[side],
            recv_sem=halo_recv.at[side], device_id=(me, above if side == 0 else below), device_id_type=MESH,
        )

    def state(i, part):
        rows = pl.ds(part * 128, 128)
        return pltpu.make_async_remote_copy(
            src_ref=mine.at[other(i), rows], dst_ref=blocked.at[me, rows], send_sem=state_send.at[part, i],
            recv_sem=state_recv.at[part, i], device_id=(other(i), tile), device_id_type=MESH,
        )

    def edge(k):
        return pltpu.make_async_remote_copy(
            src_ref=mine.at[:, pl.ds(PLACE[k] * 64, 64)], dst_ref=region.at[k], send_sem=region_send.at[k],
            recv_sem=region_recv.at[k], device_id=(me, above if k > 1 else below), device_id_type=MESH,
        )

    def seen_copy(i):
        return pltpu.make_async_remote_copy(
            src_ref=seen_out.at[other(i)], dst_ref=ob_ref.at[me], send_sem=ob_send.at[i],
            recv_sem=ob_recv.at[i], device_id=(other(i), tile), device_id_type=MESH,
        )

    for load in loads:
        load.wait()
    turn_in(x_ref, first, (0, 1, 6, 7))
    halo_out[1] = first[SPAN + 8:SPAN + 1032, :].astype(BF16)
    halo_out[0] = first[4 * SPAN + 8:4 * SPAN + 1032, :].astype(BF16)
    pl.semaphore_wait(barrier, 17)
    halo(0).start()
    halo(1).start()
    turn_in(x_ref, first, (2, 3, 4, 5))
    wrap(first, (1, 2, 3, 4))
    upper = lax.broadcasted_iota(jnp.int32, (8, 8, 128), 1) < 4
    u = 0.5 * u_ref[...][None]
    v = 0.5 * v_ref[...][None]

    def coef(y0):
        return d_ref[pl.ds(y0, 8)], u, v

    def advance(k_list, low, high):
        @pl.loop(0, 16)
        def _(step):
            y0 = step * 8
            for k, value in zip(k_list, stencil(first, k_list, low, high, y0, coef(y0), upper)):
                second[pl.ds(pl.multiple_of(k * SPAN + (y0 + 1) * 8, 8), 64), :] = value.reshape(64, 128)

    def finish(k_list, part):
        def one(b):
            y0 = b * 8
            for k, value in zip(k_list, stencil(second, k_list, 0, 5, y0, coef(y0), upper)):
                place = PLACE[k - 1] * 64
                mine[b, place:place + 64, :] = value.reshape(64, 128).astype(BF16)

        one(other(0))

        @pl.loop(1, 15)
        def _(i):
            one(other(i))
            state(i - 1, part).start()

        one(me)
        state(14, part).start()
        blocked[me, part * 128:part * 128 + 128, :] = mine[me, part * 128:part * 128 + 128, :]

    advance((1, 2, 3, 4), 1, 4)
    wrap(second, (2, 3))
    finish((2, 3), 0)
    edge(1).start()
    edge(2).start()
    for side in (0, 1):
        halo(side).wait()
        k = 5 * side
        first[k * SPAN + 8:k * SPAN + 1032, :] = halo_in[side].astype(F32)
    wrap(first, (0, 5))
    advance((0, 1, 4, 5), 0, 5)
    wrap(second, (1, 4))
    finish((1, 4), 1)
    edge(0).start()
    edge(3).start()

    cell = cell_ref[...]
    level_index = cell // 256
    rest = cell % 256
    row = rest // 16
    col = rest % 16
    half = level_index // 4
    index = (row // 2) * 128 + col * 8 + (row % 2) * 4 + level_index % 4
    lane = lax.broadcasted_iota(jnp.int32, (256, 128), 1)
    left = lane < 64

    def pick(i, kk_list):
        b = other(i)
        before, after = lax.rem(b + 15, 16), lax.rem(b + 1, 16)
        picks, pieces = [], []
        for kk in kk_list:
            picks.append(jnp.where(index[:, i:i + 1] == lane + kk * 128, 1.0, 0.0).astype(BF16))
            if 2 <= kk < 6:
                place = PLACE[kk - 2] * 64
                pieces.append(mine[before, place + 32:place + 64, :])
                pieces.append(mine[b, place:place + 64, :])
                pieces.append(mine[after, place:place + 32, :])
            else:
                k = kk + 2 if kk < 2 else kk - 6
                pieces.append(region[k, before, 32:64, :])
                pieces.append(region[k, b, :, :])
                pieces.append(region[k, after, 0:32, :])
        return nn(jnp.concatenate(picks, axis=1), jnp.concatenate(pieces, axis=0))

    for i in range(16):
        seen[i] = pick(i, (2, 3, 4, 5))
    for k in (1, 2, 0, 3):
        edge(k).wait()
    for i in range(16):
        values = seen[i] + pick(i, (0, 1, 6, 7))
        values = jnp.where((half[:, i:i + 1] == 0) == left, values, 0.0)
        values = values + pltpu.roll(values, 64, 1)
        packed = jnp.where(left[0:128], values[0:128], values[128:256]).astype(BF16)
        if i < 15:
            seen_out[other(i)] = packed
        else:
            ob_ref[me] = packed
        if i > 0:
            seen_copy(i - 1).start()

    for part in range(2):
        @pl.loop(0, 15)
        def _(i):
            state(i, part).wait()

    total = blocked[0].astype(F32)
    for g in range(1, 16):
        total = total + blocked[g].astype(F32)
    centre0 = jnp.sum(jnp.where(left, total, 0.0), axis=1, keepdims=True) * (1.0 / MEMBERS)
    centre1 = jnp.sum(jnp.where(left, 0.0, total), axis=1, keepdims=True) * (1.0 / MEMBERS)
    centre = jnp.where(left, centre0, centre1)
    centre_ref[...] = centre
    for i in range(16):
        dev_ref[:, i * 128:(i + 1) * 128] = (blocked[other(i)].astype(F32) - centre).astype(BF16)

    @pl.loop(0, 15)
    def _(i):
        seen_copy(i).wait()


def backward(
    ob_ref, dev_ref, centre_ref, weight_ref, value_ref, count_ref, out_ref, basis, sending, send_sem, recv_sem
):
    me = lax.axis_index("grp")
    tile = lax.axis_index("tile")

    def other(i):
        return lax.rem(me + 1 + i, 16)

    barrier = pltpu.get_barrier_semaphore()

    @pl.loop(0, 15)
    def _(i):
        pl.semaphore_signal(barrier, inc=1, device_id=(other(i), tile), device_id_type=MESH)

    def result(i, part):
        rows = pl.ds(part * 128, 128)
        return pltpu.make_async_remote_copy(
            src_ref=sending.at[other(i), rows], dst_ref=out_ref.at[me, rows], send_sem=send_sem.at[part, i],
            recv_sem=recv_sem.at[part, i], device_id=(other(i), tile), device_id_type=MESH,
        )

    left = lax.broadcasted_iota(jnp.int32, (128, 128), 1) < 64
    left2 = lax.broadcasted_iota(jnp.int32, (256, 128), 1) < 64
    total = ob_ref[0].astype(F32)
    for g in range(1, 16):
        total = total + ob_ref[g].astype(F32)
    mean0 = jnp.sum(jnp.where(left, total, 0.0), axis=1, keepdims=True) * (1.0 / MEMBERS)
    mean1 = jnp.sum(jnp.where(left, 0.0, total), axis=1, keepdims=True) * (1.0 / MEMBERS)
    count = count_ref[0, 0]
    row_lane = lax.broadcasted_iota(jnp.int32, (1, 128), 1)
    root0 = jnp.sqrt(jnp.where(row_lane < count, weight_ref[0:1, :], 0.0))
    root1 = jnp.sqrt(jnp.where(row_lane + 128 < count, weight_ref[1:2, :], 0.0))
    root0 = jnp.broadcast_to(root0, (128, 128)).T
    root1 = jnp.broadcast_to(root1, (128, 128)).T
    target0 = jnp.broadcast_to(value_ref[0:1, :], (128, 128)).T
    target1 = jnp.broadcast_to(value_ref[1:2, :], (128, 128)).T
    misfit = jnp.concatenate([root0 * (target0 - mean0), root1 * (target1 - mean1)], axis=0)
    mean = jnp.where(left, mean0, mean1)
    root = jnp.where(left, root0, root1)
    for i in range(16):
        scaled = (ob_ref[other(i)].astype(F32) - mean) * root
        turned = pltpu.roll(scaled, 64, 1)
        both = jnp.concatenate(
            [jnp.where(left, scaled, turned), jnp.where(left, turned, scaled)], axis=0
        )
        basis[0:256, i * 128:(i + 1) * 128] = jnp.where(left2, both, 0.0).astype(BF16)
        basis[256:512, i * 128:(i + 1) * 128] = jnp.where(left2, 0.0, both).astype(BF16)
    small = nt(basis[0:256, :], basis[0:256, :])
    eye = lax.broadcasted_iota(jnp.int32, (256, 256), 0) == lax.broadcasted_iota(jnp.int32, (256, 256), 1)
    trace = jnp.sum(jnp.where(eye, small, 0.0), axis=(0, 1), keepdims=True)
    s = (MEMBERS - 1.0) + trace * (1.0 / MEMBERS)
    inv_s = 1.0 / s
    inv_root_s = lax.rsqrt(s)
    a = (MEMBERS - 1.0) * inv_s
    p = 1.5 - 0.5 * a
    r0 = 1.5 * p - 0.5 * a * p * p * p
    r1 = -0.75 - 0.5 * p * p * p + 0.75 * a * p * p
    r2 = 0.5 * (1.5 * p * p - 0.75 * a * p)
    r3 = (1.0 / 6.0) * (0.375 * a - 2.25 * p)
    r4 = 1.5 / 24.0
    g1 = small * inv_s
    g2 = nn(g1, g1, HIGH)
    q = jnp.where(eye, r1, 0.0) + r2 * g1 + r3 * g2 + r4 * nn(g2, g1, HIGH)
    first = (r0 * misfit + nn(g1, nn(q, misfit, HIGH), HIGH)) * inv_root_s
    gain = (r0 * first + nn(g1, nn(q, first, HIGH), HIGH)) * inv_root_s
    spread = jnp.sqrt(jnp.full((1, 1), MEMBERS - 1.0, F32))
    mix = q * (spread * inv_s * inv_root_s)
    keep = r0 * spread * inv_root_s
    cross = nt(dev_ref[...], basis[...])
    cross0, cross1 = cross[:, 0:256], cross[:, 256:512]
    update = jnp.concatenate([nn(cross0, mix, HIGH), nn(cross1, mix, HIGH)], axis=1).astype(BF16)
    offset = centre_ref[...] + jnp.where(left2, nn(cross0, gain, HIGH), nn(cross1, gain, HIGH))
    pl.semaphore_wait(barrier, 15)
    for part in range(2):
        rows = slice(part * 128, part * 128 + 128)
        for i in range(16):
            lanes = slice(i * 128, (i + 1) * 128)
            value = offset[rows] + keep * dev_ref[rows, lanes].astype(F32) + nn(update[rows], basis[:, lanes])
            if i < 15:
                sending[other(i), rows, :] = value.astype(BF16)
            else:
                out_ref[me, rows, :] = value.astype(BF16)
            if i > 0:
                result(i - 1, part).start()
    for part in range(2):
        @pl.loop(0, 15)
        def _(i):
            result(i, part).wait()


def turn_out(r_ref, out_ref, field, stage):
    for b in range(16):
        for place in range(4):
            field[pl.ds(PAIR[place] * 1024 + b * 64, 64), :] = r_ref[b, place * 64:(place + 1) * 64, :].astype(F32)
    for row in range(8):
        for level in range(4):
            start = level * 8 + row
            plane = field[pl.ds((row // 2) * 1024 + (row % 2) * 4 + level, 128, stride=8), :].T
            stage[pl.ds(start, 64, stride=64), :] = plane[0:64]
            stage[pl.ds(start + 32, 64, stride=64), :] = plane[64:128]
    out_ref[...] = stage[...].astype(BF16)


def params(collective=None, mib=30):
    if collective is None:
        return pltpu.CompilerParams(vmem_limit_bytes=mib * 1024 * 1024)
    return pltpu.CompilerParams(
        vmem_limit_bytes=mib * 1024 * 1024, collective_id=collective, has_side_effects=True
    )


def call_forward(x, d, u, v, cell):
    dma = pltpu.SemaphoreType.DMA
    return pl.pallas_call(
        forward,
        out_shape=(
            jax.ShapeDtypeStruct((16, 128, 128), BF16),
            jax.ShapeDtypeStruct((256, 2048), BF16),
            jax.ShapeDtypeStruct((256, 128), F32),
        ),
        in_specs=[ANY, VMEM, VMEM, VMEM, VMEM],
        out_specs=(VMEM, VMEM, VMEM),
        scratch_shapes=[
            pltpu.VMEM((4, 1024, 128), F32),
            pltpu.VMEM((6 * SPAN, 128), F32),
            pltpu.VMEM((6 * SPAN, 128), F32),
            pltpu.VMEM((2, 1024, 128), BF16),
            pltpu.VMEM((2, 1024, 128), BF16),
            pltpu.VMEM((16, 256, 128), BF16),
            pltpu.VMEM((16, 256, 128), BF16),
            pltpu.VMEM((4, 16, 64, 128), BF16),
            pltpu.VMEM((16, 256, 128), F32),
            pltpu.VMEM((16, 128, 128), BF16),
            dma((4,)), dma((2,)), dma((2,)), dma((2, 15)), dma((2, 15)), dma((4,)), dma((4,)), dma((15,)), dma((15,)),
        ],
        compiler_params=params(0),
        name="forward",
    )(x, d, u, v, cell)


def call_backward(ob, dev, centre, weight, value, count):
    dma = pltpu.SemaphoreType.DMA
    return pl.pallas_call(
        backward,
        out_shape=jax.ShapeDtypeStruct((16, 256, 128), BF16),
        in_specs=[VMEM, VMEM, VMEM, VMEM, VMEM, SMEM],
        out_specs=VMEM,
        scratch_shapes=[
            pltpu.VMEM((512, 2048), BF16),
            pltpu.VMEM((16, 256, 128), BF16),
            dma((2, 15)), dma((2, 15)),
        ],
        compiler_params=params(1),
        name="backward",
    )(ob, dev, centre, weight, value, count)


def call_turn_out(r):
    return pl.pallas_call(
        turn_out,
        out_shape=jax.ShapeDtypeStruct((4096, 128), BF16),
        in_specs=[VMEM],
        out_specs=VMEM,
        scratch_shapes=[pltpu.VMEM((4096, 128), F32), pltpu.VMEM((4096, 128), F32)],
        compiler_params=params(),
        name="turn_out",
    )(r)


def coefficients(diffusivity, eastward_velocity, northward_velocity):
    d = jnp.broadcast_to(jnp.concatenate([diffusivity, diffusivity], 0).T[:, :, None], (128, 8, 128))
    u = jnp.broadcast_to(jnp.concatenate([eastward_velocity] * 2)[:, None], (8, 128))
    v = jnp.broadcast_to(jnp.concatenate([northward_velocity] * 2)[:, None], (8, 128))
    return d, u, v


def on_device(
    starting_realizations,
    diffusivity,
    eastward_velocity,
    northward_velocity,
    obs_cell,
    obs_count,
    obs_value,
    obs_weight,
):
    d, u, v = coefficients(diffusivity, eastward_velocity, northward_velocity)
    cell = obs_cell[0]
    cell = lax.dynamic_slice_in_dim(jnp.concatenate([cell, cell]), lax.axis_index("grp") + 1, 16, 0).T
    measured, deviation, centre = call_forward(starting_realizations.reshape(128, 4, 8, 128), d, u, v, cell)
    updated = call_backward(
        measured, deviation, centre, obs_weight.reshape(2, 128), obs_value.reshape(2, 128), obs_count
    )
    return call_turn_out(updated).reshape(64, 2, 4, 8, 128)


def solution(mesh):
    return jax.shard_map(
        on_device,
        mesh=mesh,
        in_specs=(
            P("grp", None, None, "tile", None),
            P(),
            P(),
            P(),
            P("tile", None, None),
            P("tile", "grp"),
            P("tile", "grp", None),
            P("tile", "grp", None),
        ),
        out_specs=P("grp", None, None, "tile", None),
        check_vma=False,
    )
```

```python
import jax
import jax.numpy as jnp
from jax import lax
from jax.experimental import pallas as pl
from jax.experimental.pallas import tpu as pltpu
from jax.sharding import PartitionSpec as P


F32 = jnp.float32
BF16 = jnp.bfloat16
VMEM = pl.BlockSpec(memory_space=pltpu.VMEM)
MEMBERS = 1024.0
MESH = pl.DeviceIdType.MESH
ANY = pl.BlockSpec(memory_space=pl.ANY)
PLACE = (2, 0, 1, 3)
PAIR = (1, 2, 0, 3)
SPAN = 130 * 8


def nt(a, b):
    return lax.dot_general(a, b, (((1,), (1,)), ((), ())), preferred_element_type=F32)


def nn(a, b):
    return lax.dot_general(a, b, (((1,), (0,)), ((), ())), preferred_element_type=F32)


def split(a):
    top = a.astype(BF16)
    return top, (a - top.astype(F32)).astype(BF16)


def nn3(a, b):
    (a0, a1), (b0, b1) = a, b
    return nn(jnp.concatenate([a0, a0, a1], axis=1), jnp.concatenate([b0, b1, b0], axis=0))


def stencil(ref, k_list, low, high, y0, coef, upper):
    d, u, v = coef
    east_c, west_c, north_c, south_c = d - u, d + u, d - v, d + v
    mid_c = 1.0 - 4.0 * d

    def rows(k, shift):
        return ref[pl.ds(pl.multiple_of(k * SPAN + (y0 + 1 + shift) * 8, 8), 64), :].reshape(8, 8, 128)

    rolled = {}

    def roll(k):
        if k not in rolled:
            rolled[k] = pltpu.roll(rows(k, 0), 4, 1)
        return rolled[k]

    outs = []
    for k in k_list:
        east = jnp.where(upper, roll(k), roll(k + 1)) if k < high else roll(k)
        west = jnp.where(upper, roll(k - 1), roll(k)) if k > low else roll(k)
        outs.append(
            rows(k, 0) * mid_c + east * east_c + west * west_c + rows(k, 1) * north_c + rows(k, -1) * south_c
        )
    return outs


def wrap(ref, k_list):
    for k in k_list:
        ref[k * SPAN:k * SPAN + 8, :] = ref[k * SPAN + 1024:k * SPAN + 1032, :]
        ref[k * SPAN + 1032:k * SPAN + 1040, :] = ref[k * SPAN + 8:k * SPAN + 16, :]


def turn_in(x_ref, field, rows):
    for row in rows:
        for level in range(4):
            start = level * 8 + row
            plane = jnp.concatenate(
                [x_ref[pl.ds(start, 64, stride=64), :], x_ref[pl.ds(start + 32, 64, stride=64), :]], axis=0
            )
            start = (row // 2 + 1) * SPAN + 8 + (row % 2) * 4 + level
            field[pl.ds(start, 128, stride=8), :] = plane.T


def turn_out(returned, field, stage, place):
    k = PAIR[place]
    for b in range(16):
        field[k * 1024 + b * 64:k * 1024 + b * 64 + 64, :] = returned[b, place * 64:place * 64 + 64, :].astype(F32)
    for row in (2 * k, 2 * k + 1):
        for level in range(4):
            start = level * 8 + row
            plane = field[pl.ds(k * 1024 + (row % 2) * 4 + level, 128, stride=8), :].T
            stage[pl.ds(start, 64, stride=64), :] = plane[0:64]
            stage[pl.ds(start + 32, 64, stride=64), :] = plane[64:128]


def whole(
    x_hbm, d_hbm, u_hbm, v_hbm, cell_hbm, weight_hbm, value_hbm, count_ref, out_ref,
    d_ref, u_ref, v_ref, cell_ref, weight_ref, value_ref, small_sem, x_ref, first, second, spread_d, cells, hot, halo_out, halo_in, mine, blocked, region, seen, seen_out, measured,
    dev, basis, sending, returned,
    load_sem, halo_send, halo_recv, state_send, state_recv, late_send, late_recv, region_send, region_recv,
    ob_send, ob_recv, back_send, back_recv,
):
    me = lax.axis_index("grp")
    tile = lax.axis_index("tile")
    tiles = lax.axis_size("tile")
    below, above = lax.rem(tile + tiles - 1, tiles), lax.rem(tile + 1, tiles)

    def other(i):
        return lax.rem(me + 1 + i, 16)

    small_loads = []
    for source, target in (
        (d_hbm, d_ref), (u_hbm, u_ref), (v_hbm, v_ref), (cell_hbm, cell_ref), (weight_hbm, weight_ref),
        (value_hbm, value_ref),
    ):
        small_loads.append(pltpu.make_async_copy(source, target, small_sem.at[len(small_loads)]))
        small_loads[-1].start()
    loads = []
    for piece in range(4):
        rows = pl.ds(piece * 1024, 1024)
        loads.append(pltpu.make_async_copy(x_hbm.at[rows], x_ref.at[rows], load_sem.at[piece]))
        loads[-1].start()
    barrier = pltpu.get_barrier_semaphore()

    @pl.loop(0, 15)
    def _(i):
        pl.semaphore_signal(barrier, inc=1, device_id=(other(i), tile), device_id_type=MESH)

    pl.semaphore_signal(barrier, inc=1, device_id=(me, below), device_id_type=MESH)
    pl.semaphore_signal(barrier, inc=1, device_id=(me, above), device_id_type=MESH)

    def remote(source, target, send, recv, device):
        return pltpu.make_async_remote_copy(
            src_ref=source, dst_ref=target, send_sem=send, recv_sem=recv, device_id=device, device_id_type=MESH
        )

    def halo(side):
        return remote(
            halo_out.at[side], halo_in.at[side], halo_send.at[side], halo_recv.at[side],
            (me, above if side == 0 else below),
        )

    def state(i):
        rows = pl.ds(0, 128)
        return remote(
            mine.at[other(i), rows], blocked.at[me, rows], state_send.at[i], state_recv.at[i], (other(i), tile)
        )

    def late(i, part):
        rows = pl.ds(128 + 64 * part, 64)
        return remote(
            mine.at[other(i), rows], blocked.at[me, rows], late_send.at[part, i], late_recv.at[part, i],
            (other(i), tile),
        )

    def edge(k):
        return remote(
            mine.at[:, pl.ds(PLACE[k] * 64, 64)], region.at[k], region_send.at[k], region_recv.at[k],
            (me, above if k > 1 else below),
        )

    def seen_copy(i):
        return remote(seen_out.at[other(i)], measured.at[me], ob_send.at[i], ob_recv.at[i], (other(i), tile))

    def back(i, place):
        rows = pl.ds(place * 64, 64)
        return remote(
            sending.at[other(i), rows], returned.at[me, rows], back_send.at[place, i], back_recv.at[place, i],
            (other(i), tile),
        )

    for load in loads:
        load.wait()
    turn_in(x_ref, first, (0, 1, 6, 7))
    halo_out[1] = first[SPAN + 8:SPAN + 1032, :].astype(BF16)
    halo_out[0] = first[4 * SPAN + 8:4 * SPAN + 1032, :].astype(BF16)
    pl.semaphore_wait(barrier, 17)
    halo(0).start()
    halo(1).start()

    for load in small_loads:
        load.wait()
    sub = lax.broadcasted_iota(jnp.int32, (8, 128), 0)
    u = jnp.zeros((8, 128), F32)
    v = jnp.zeros((8, 128), F32)
    for level in range(4):
        column = jnp.broadcast_to(d_ref[level:level + 1, :], (128, 128)).T
        spread_d[pl.ds(level, 128, stride=8), :] = column
        spread_d[pl.ds(level + 4, 128, stride=8), :] = column
        here = lax.rem(sub, 4) == level
        u = jnp.where(here, 0.5 * u_ref[level], u)
        v = jnp.where(here, 0.5 * v_ref[level], v)
    turn_in(x_ref, first, (2, 3, 4, 5))
    wrap(first, (1, 2, 3, 4))
    upper = lax.broadcasted_iota(jnp.int32, (8, 8, 128), 1) < 4

    def coef(y0):
        return spread_d[pl.ds(pl.multiple_of(y0 * 8, 64), 64), :].reshape(8, 8, 128), u[None], v[None]

    def finish(k_list, send, before=None):
        def one(b):
            y0 = b * 8
            for k, value in zip(k_list, stencil(second, k_list, 0, 5, y0, coef(y0), upper)):
                place = PLACE[k - 1] * 64
                mine[b, place:place + 64, :] = value.reshape(64, 128).astype(BF16)

        one(other(0))

        @pl.loop(1, 14)
        def _(i):
            if before is not None:
                before(i + 2)
            one(other(i))
            send(i - 1).start()

        one(other(14))
        send(13).start()
        one(me)
        send(14).start()

    def inner(ahead):
        block = lax.rem(me + ahead, 16)
        y0 = block * 8
        for k, value in zip((1, 2, 3, 4), stencil(first, (1, 2, 3, 4), 1, 4, y0, coef(y0), upper)):
            second[pl.ds(pl.multiple_of(k * SPAN + (y0 + 1) * 8, 8), 64), :] = value.reshape(64, 128)

        @pl.when(block == 0)
        def _():
            for k in (2, 3):
                second[k * SPAN + 1032:k * SPAN + 1040, :] = second[k * SPAN + 8:k * SPAN + 16, :]

        @pl.when(block == 15)
        def _():
            for k in (2, 3):
                second[k * SPAN:k * SPAN + 8, :] = second[k * SPAN + 1024:k * SPAN + 1032, :]

    @pl.loop(0, 3)
    def _(ahead):
        inner(ahead)

    finish((2, 3), state, inner)
    edge(1).start()
    edge(2).start()

    for i in range(16):
        cell = cell_ref[pl.ds(other(i), 1), :]
        place = cell % 256
        row, col = place // 16, place % 16
        level = cell // 256
        pair = row // 2
        own = (pair >= 2) & (pair <= 5)
        group = jnp.where(own, (pair - 2) // 2, jnp.where((pair == 0) | (pair == 7), 2, 3))
        second_of = jnp.where(own, pair % 2, jnp.where(pair >= 6, 1, 0))
        cells[0, i:i + 1, :] = (second_of * 128 + col * 8 + (row % 2) * 4 + level % 4).astype(F32)
        cells[1, i:i + 1, :] = (group + 4 * (level // 4)).astype(F32)
    index = jnp.concatenate([cells[0, :, 0:128].T, cells[0, :, 128:256].T], axis=0)
    choice = jnp.concatenate([cells[1, :, 0:128].T, cells[1, :, 128:256].T], axis=0)
    count = count_ref[0, 0]
    row_lane = lax.broadcasted_iota(jnp.int32, (1, 128), 1)
    root_rows, roots = [], []
    for part in range(2):
        root = jnp.sqrt(jnp.where(row_lane + 128 * part < count, weight_ref[part:part + 1, :], 0.0))
        root_rows.append(root)
        roots.append(jnp.broadcast_to(root, (128, 128)).T)

    for side in (0, 1):
        halo(side).wait()
        k = 5 * side
        first[k * SPAN + 8:k * SPAN + 1032, :] = halo_in[side].astype(F32)
    wrap(first, (0, 5))

    @pl.loop(0, 16)
    def _(step):
        y0 = step * 8
        d, u_c, v_c = coef(y0)
        for upper_k, lower_k, east_k, west_k, own in ((1, 0, 1, 0, 1), (5, 4, 5, 4, 4)):
            def rows(k, shift):
                return first[pl.ds(pl.multiple_of(k * SPAN + (y0 + 1 + shift) * 8, 8), 64), :].reshape(8, 8, 128)

            def mixed(shift):
                return jnp.where(upper, rows(upper_k, shift), rows(lower_k, shift))

            east = pltpu.roll(rows(east_k, 0), 4, 1)
            west = pltpu.roll(rows(west_k, 0), 4, 1)
            value = (
                mixed(0) * (1.0 - 4.0 * d) + east * (d - u_c) + west * (d + u_c)
                + mixed(1) * (d - v_c) + mixed(-1) * (d + v_c)
            )
            own_rows = pl.ds(pl.multiple_of(own * SPAN + (y0 + 1) * 8, 8), 64)
            kept = second[own_rows, :].reshape(8, 8, 128)
            kept = jnp.where(upper, value, kept) if own == 1 else jnp.where(upper, kept, value)
            second[own_rows, :] = kept.reshape(64, 128)
            side_k = 0 if own == 1 else 5
            second[pl.ds(pl.multiple_of(side_k * SPAN + (y0 + 1) * 8, 8), 64), :] = value.reshape(64, 128)

    wrap(second, (1, 4))
    finish((1, 4), lambda i: late(i, 0))
    edge(0).start()
    edge(3).start()
    blocked[me] = mine[me]

    lane = lax.broadcasted_iota(jnp.int32, (256, 128), 1)
    lane_f = lane.astype(F32)
    left2 = lane < 64
    left = left2[0:128]

    lane_choice = jnp.where(left2, 0.0, 4.0)

    def picked(i, pairs):
        b = other(i)
        before, after = lax.rem(b + 15, 16), lax.rem(b + 1, 16)
        columns = []
        for group in pairs:
            pieces = []
            for kk in group:
                if 2 <= kk < 6:
                    place = PLACE[kk - 2] * 64
                    pieces.append(mine[before, place + 32:place + 64, :])
                    pieces.append(mine[b, place:place + 64, :])
                    pieces.append(mine[after, place:place + 32, :])
                else:
                    k = kk + 2 if kk < 2 else kk - 6
                    pieces.append(region[k, before, 32:64, :])
                    pieces.append(region[k, b, :, :])
                    pieces.append(region[k, after, 0:32, :])
            columns.append(jnp.concatenate(pieces, axis=0))
        return nn(hot[i], jnp.concatenate(columns, axis=1))

    for i in range(16):
        here = jnp.broadcast_to(index[:, i:i + 1], (256, 128))
        hot[i, :, 0:128] = jnp.where(here == lane_f, 1.0, 0.0).astype(BF16)
        hot[i, :, 128:256] = jnp.where(here == lane_f + 128.0, 1.0, 0.0).astype(BF16)
        values = picked(i, ((2, 3), (4, 5)))
        wanted = choice[:, i:i + 1] - lane_choice
        seen[i] = jnp.where(wanted == 0.0, values[:, 0:128], jnp.where(wanted == 1.0, values[:, 128:256], 0.0))
    for k in (1, 2, 0, 3):
        edge(k).wait()
    for i in range(16):
        values = picked(i, ((0, 7), (1, 6)))
        wanted = choice[:, i:i + 1] - lane_choice
        values = jnp.where(wanted == 2.0, values[:, 0:128], jnp.where(wanted == 3.0, values[:, 128:256], seen[i]))
        values = values + pltpu.roll(values, 64, 1)
        packed = jnp.where(left, values[0:128], values[128:256]).astype(BF16)
        if i < 15:
            seen_out[other(i)] = packed
        else:
            measured[me] = packed
        if i > 0:
            seen_copy(i - 1).start()

    @pl.loop(0, 15)
    def _(i):
        late(i, 1).start()

    def centred(start, count):
        rows = slice(start, start + count)
        left_rows = left2[rows]
        total = blocked[0, rows, :].astype(F32)
        for g in range(1, 16):
            total = total + blocked[g, rows, :].astype(F32)
        centre0 = jnp.sum(jnp.where(left_rows, total, 0.0), axis=1, keepdims=True) * (1.0 / MEMBERS)
        centre1 = jnp.sum(jnp.where(left_rows, 0.0, total), axis=1, keepdims=True) * (1.0 / MEMBERS)
        centre = jnp.where(left_rows, centre0, centre1)
        target = (start // 128) * 256 + start % 128
        for q in range(8):
            even = blocked[other(2 * q), rows, :].astype(F32) - centre
            odd = blocked[other(2 * q + 1), rows, :].astype(F32) - centre
            lanes = slice(q * 128, (q + 1) * 128)
            dev[target:target + count, lanes] = jnp.where(left_rows, even, pltpu.roll(odd, 64, 1)).astype(BF16)
            dev[target + 128:target + 128 + count, lanes] = jnp.where(
                left_rows, pltpu.roll(even, 64, 1), odd
            ).astype(BF16)
        return centre0, centre1

    @pl.loop(0, 15)
    def _(i):
        state(i).wait()

    centre_a = centred(0, 128)

    @pl.loop(0, 15)
    def _(i):
        late(i, 0).wait()

    centre_b = centred(128, 64)

    @pl.loop(0, 15)
    def _(i):
        seen_copy(i).wait()

    total = measured[0].astype(F32)
    for g in range(1, 16):
        total = total + measured[g].astype(F32)
    mean0 = jnp.sum(jnp.where(left, total, 0.0), axis=1, keepdims=True) * (1.0 / MEMBERS)
    mean1 = jnp.sum(jnp.where(left, 0.0, total), axis=1, keepdims=True) * (1.0 / MEMBERS)
    misfit = jnp.concatenate(
        [
            root_rows[part] * (value_ref[part:part + 1, :] - jnp.broadcast_to(mean, (128, 128)).T[0:16])
            for part, mean in enumerate((mean0, mean1))
        ],
        axis=1,
    )
    mean = jnp.where(left, mean0, mean1)
    root = jnp.where(left, roots[0], roots[1])
    for q in range(8):
        even = (measured[other(2 * q)].astype(F32) - mean) * root
        odd = (measured[other(2 * q + 1)].astype(F32) - mean) * root
        lanes = slice(q * 128, (q + 1) * 128)
        basis[0:128, lanes] = jnp.where(left, even, pltpu.roll(odd, 64, 1)).astype(BF16)
        basis[128:256, lanes] = jnp.where(left, pltpu.roll(even, 64, 1), odd).astype(BF16)
    small = nt(basis[...], basis[...])
    eye = lax.broadcasted_iota(jnp.int32, (256, 256), 0) == lax.broadcasted_iota(jnp.int32, (256, 256), 1)
    trace = jnp.sum(jnp.where(eye, small, 0.0), axis=(0, 1), keepdims=True)
    s = (MEMBERS - 1.0) + trace * (1.0 / MEMBERS)
    inv_s = 1.0 / s
    inv_root_s = lax.rsqrt(s)
    a = (MEMBERS - 1.0) * inv_s
    p = 1.5 - 0.5 * a
    r0 = 1.5 * p - 0.5 * a * p * p * p
    r1 = -0.75 - 0.5 * p * p * p + 0.75 * a * p * p
    r2 = 0.5 * (1.5 * p * p - 0.75 * a * p)
    r3 = (1.0 / 6.0) * (0.375 * a - 2.25 * p)
    r4 = 1.5 / 24.0
    spread = jnp.sqrt(jnp.full((1, 1), MEMBERS - 1.0, F32))
    keep = r0 * spread * inv_root_s
    g1 = small * inv_s
    g1_s = split(g1)
    g2 = nn3(g1_s, g1_s)
    g2_s = split(g2)
    g3 = nn3(g2_s, g1_s)
    g4 = nn3(g2_s, g2_s)
    mix = (jnp.where(eye, r1, 0.0) + r2 * g1 + r3 * g2 + r4 * g3) * (spread * inv_s * inv_root_s)
    step_s = split((jnp.where(eye, r0, 0.0) + r1 * g1 + r2 * g2 + r3 * g3 + r4 * g4) * inv_root_s)
    gain = nn3(split(nn3(split(misfit), step_s)), step_s)[0:1]
    mix_s = split(mix)

    def answer(part, centre):
        here = slice(part * 256, part * 256 + 256)
        rows = slice(part * 128, part * 128 + 128)
        cross = nt(dev[here, :], basis[...])
        update = nn3(split(cross), mix_s).astype(BF16)
        offset = centre + jnp.sum(cross * gain, axis=1, keepdims=True)
        for double in range(4):
            lanes = slice(double * 256, double * 256 + 256)
            both = offset + keep * dev[here, lanes].astype(F32) + nn(update, basis[:, lanes])
            for q in (2 * double, 2 * double + 1):
                value = both[:, 0:128] if q % 2 == 0 else both[:, 128:256]
                var0, var1 = value[0:128], value[128:256]
                sending[other(2 * q), rows, :] = jnp.where(left, var0, pltpu.roll(var1, 64, 1)).astype(BF16)
                odd = jnp.where(left, pltpu.roll(var0, 64, 1), var1).astype(BF16)
                if q < 7:
                    sending[other(2 * q + 1), rows, :] = odd
                else:
                    returned[me, rows, :] = odd
                if q > 0:
                    back(2 * q - 2, 2 * part).start()
                    back(2 * q - 1, 2 * part).start()
        back(14, 2 * part).start()

        @pl.loop(0, 15)
        def _(i):
            back(i, 2 * part + 1).start()

    answer(0, jnp.concatenate(centre_a, axis=0))

    @pl.loop(0, 15)
    def _(i):
        late(i, 1).wait()

    centre_c = centred(192, 64)
    answer(1, jnp.concatenate([centre_b[0], centre_c[0], centre_b[1], centre_c[1]], axis=0))

    for place in range(4):
        @pl.loop(0, 15)
        def _(i):
            back(i, place).wait()

        turn_out(returned, first, second, place)
    out_ref[...] = second[0:4096, :].astype(BF16)


def call_whole(x, d, u, v, cell, weight, value, count):
    dma = pltpu.SemaphoreType.DMA
    return pl.pallas_call(
        whole,
        out_shape=jax.ShapeDtypeStruct((4096, 128), BF16),
        in_specs=[ANY] * 7 + [pl.BlockSpec(memory_space=pltpu.SMEM)],
        out_specs=VMEM,
        scratch_shapes=[
            pltpu.VMEM((4, 128), F32),
            pltpu.SMEM((4,), F32),
            pltpu.SMEM((4,), F32),
            pltpu.VMEM((16, 256), jnp.int32),
            pltpu.VMEM((2, 128), F32),
            pltpu.VMEM((2, 128), F32),
            dma((6,)),
            pltpu.VMEM((4096, 128), F32),
            pltpu.VMEM((6 * SPAN, 128), F32),
            pltpu.VMEM((6 * SPAN, 128), F32),
            pltpu.VMEM((1024, 128), F32),
            pltpu.VMEM((2, 128, 256), F32),
            pltpu.VMEM((16, 256, 256), BF16),
            pltpu.VMEM((2, 1024, 128), BF16),
            pltpu.VMEM((2, 1024, 128), BF16),
            pltpu.VMEM((16, 256, 128), BF16),
            pltpu.VMEM((16, 256, 128), BF16),
            pltpu.VMEM((4, 16, 64, 128), BF16),
            pltpu.VMEM((16, 256, 128), F32),
            pltpu.VMEM((16, 128, 128), BF16),
            pltpu.VMEM((16, 128, 128), BF16),
            pltpu.VMEM((512, 1024), BF16),
            pltpu.VMEM((256, 1024), BF16),
            pltpu.VMEM((16, 256, 128), BF16),
            pltpu.VMEM((16, 256, 128), BF16),
            dma((4,)), dma((2,)), dma((2,)), dma((15,)), dma((15,)), dma((2, 15)), dma((2, 15)), dma((4,)), dma((4,)),
            dma((15,)), dma((15,)), dma((4, 15)), dma((4, 15)),
        ],
        compiler_params=pltpu.CompilerParams(
            vmem_limit_bytes=48000000, collective_id=0, has_side_effects=True
        ),
        name="whole",
    )(x, d, u, v, cell, weight, value, count)


def hbm(x):
    return pltpu.with_memory_space_constraint(x, pltpu.MemorySpace.HBM)


def on_device(
    starting_realizations,
    diffusivity,
    eastward_velocity,
    northward_velocity,
    obs_cell,
    obs_count,
    obs_value,
    obs_weight,
):
    analysis = call_whole(
        hbm(starting_realizations.reshape(4096, 128)), hbm(diffusivity), hbm(eastward_velocity), hbm(northward_velocity),
        hbm(obs_cell[0]), hbm(obs_weight.reshape(2, 128)), hbm(obs_value.reshape(2, 128)), obs_count,
    )
    return analysis.reshape(64, 2, 4, 8, 128)


def solution(mesh):
    return jax.shard_map(
        on_device,
        mesh=mesh,
        in_specs=(
            P("grp", None, None, "tile", None),
            P(),
            P(),
            P(),
            P("tile", None, None),
            P("tile", "grp"),
            P("tile", "grp", None),
            P("tile", "grp", None),
        ),
        out_specs=P("grp", None, None, "tile", None),
        check_vma=False,
    )
```

```python
import jax
import jax.numpy as jnp
from jax import lax
from jax.experimental import pallas as pl
from jax.experimental.pallas import tpu as pltpu
from jax.sharding import PartitionSpec as P


F32 = jnp.float32
BF16 = jnp.bfloat16
VMEM = pl.BlockSpec(memory_space=pltpu.VMEM)
MEMBERS = 1024.0
MESH = pl.DeviceIdType.MESH
ANY = pl.BlockSpec(memory_space=pl.ANY)
PLACE = (2, 0, 1, 3)
PAIR = (1, 2, 0, 3)
SPAN = 130 * 8


def nt(a, b):
    return lax.dot_general(a, b, (((1,), (1,)), ((), ())), preferred_element_type=F32)


def nn(a, b):
    return lax.dot_general(a, b, (((1,), (0,)), ((), ())), preferred_element_type=F32)


def split(a):
    top = a.astype(BF16)
    return top, (a - top.astype(F32)).astype(BF16)


def nn3(a, b):
    (a0, a1), (b0, b1) = a, b
    return nn(jnp.concatenate([a0, a0, a1], axis=1), jnp.concatenate([b0, b1, b0], axis=0))


def stencil(ref, k_list, low, high, y0, coef, upper):
    d, u, v = coef
    east_c, west_c, north_c, south_c = d - u, d + u, d - v, d + v
    mid_c = 1.0 - 4.0 * d

    def rows(k, shift):
        return ref[pl.ds(pl.multiple_of(k * SPAN + (y0 + 1 + shift) * 8, 8), 64), :].reshape(8, 8, 128)

    rolled = {}

    def roll(k):
        if k not in rolled:
            rolled[k] = pltpu.roll(rows(k, 0), 4, 1)
        return rolled[k]

    outs = []
    for k in k_list:
        east = jnp.where(upper, roll(k), roll(k + 1)) if k < high else roll(k)
        west = jnp.where(upper, roll(k - 1), roll(k)) if k > low else roll(k)
        outs.append(
            rows(k, 0) * mid_c + east * east_c + west * west_c + rows(k, 1) * north_c + rows(k, -1) * south_c
        )
    return outs


def wrap(ref, k_list):
    for k in k_list:
        ref[k * SPAN:k * SPAN + 8, :] = ref[k * SPAN + 1024:k * SPAN + 1032, :]
        ref[k * SPAN + 1032:k * SPAN + 1040, :] = ref[k * SPAN + 8:k * SPAN + 16, :]


def turn_in(x_ref, field, rows):
    for row in rows:
        for level in range(4):
            start = level * 8 + row
            plane = jnp.concatenate(
                [x_ref[pl.ds(start, 64, stride=64), :], x_ref[pl.ds(start + 32, 64, stride=64), :]], axis=0
            )
            start = (row // 2 + 1) * SPAN + 8 + (row % 2) * 4 + level
            field[pl.ds(start, 128, stride=8), :] = plane.T


def turn_out(returned, field, stage, place):
    k = PAIR[place]
    for b in range(16):
        field[k * 1024 + b * 64:k * 1024 + b * 64 + 64, :] = returned[b, place * 64:place * 64 + 64, :].astype(F32)
    for row in (2 * k, 2 * k + 1):
        for level in range(4):
            start = level * 8 + row
            plane = field[pl.ds(k * 1024 + (row % 2) * 4 + level, 128, stride=8), :].T
            stage[pl.ds(start, 64, stride=64), :] = plane[0:64]
            stage[pl.ds(start + 32, 64, stride=64), :] = plane[64:128]


def whole(
    x_hbm, d_hbm, u_hbm, v_hbm, cell_hbm, weight_hbm, value_hbm, count_ref, out_ref,
    d_ref, u_ref, v_ref, cell_ref, weight_ref, value_ref, small_sem, x_ref, first, second, spread_d, cells, hot, halo_out, halo_in, mine, blocked, region, seen, seen_out, measured,
    dev, basis, sending, returned,
    load_sem, halo_send, halo_recv, state_send, state_recv, late_send, late_recv, region_send, region_recv,
    strip_send, strip_recv, ob_send, ob_recv, back_send, back_recv,
):
    me = lax.axis_index("grp")
    tile = lax.axis_index("tile")
    tiles = lax.axis_size("tile")
    below, above = lax.rem(tile + tiles - 1, tiles), lax.rem(tile + 1, tiles)

    def other(i):
        return lax.rem(me + 1 + i, 16)

    small_loads = []
    for source, target in (
        (d_hbm, d_ref), (u_hbm, u_ref), (v_hbm, v_ref), (cell_hbm, cell_ref), (weight_hbm, weight_ref),
        (value_hbm, value_ref),
    ):
        small_loads.append(pltpu.make_async_copy(source, target, small_sem.at[len(small_loads)]))
        small_loads[-1].start()
    loads = []
    for piece in range(4):
        rows = pl.ds(piece * 1024, 1024)
        loads.append(pltpu.make_async_copy(x_hbm.at[rows], x_ref.at[rows], load_sem.at[piece]))
        loads[-1].start()
    barrier = pltpu.get_barrier_semaphore()

    @pl.loop(0, 15)
    def _(i):
        pl.semaphore_signal(barrier, inc=1, device_id=(other(i), tile), device_id_type=MESH)

    pl.semaphore_signal(barrier, inc=1, device_id=(me, below), device_id_type=MESH)
    pl.semaphore_signal(barrier, inc=1, device_id=(me, above), device_id_type=MESH)

    def remote(source, target, send, recv, device):
        return pltpu.make_async_remote_copy(
            src_ref=source, dst_ref=target, send_sem=send, recv_sem=recv, device_id=device, device_id_type=MESH
        )

    def halo(side):
        return remote(
            halo_out.at[side], halo_in.at[side], halo_send.at[side], halo_recv.at[side],
            (me, above if side == 0 else below),
        )

    def state(i):
        rows = pl.ds(0, 128)
        return remote(
            mine.at[other(i), rows], blocked.at[me, rows], state_send.at[i], state_recv.at[i], (other(i), tile)
        )

    def late(i, part):
        rows = pl.ds(128 + 64 * part, 64)
        return remote(
            mine.at[other(i), rows], blocked.at[me, rows], late_send.at[part, i], late_recv.at[part, i],
            (other(i), tile),
        )

    def edge(k):
        return remote(
            mine.at[:, pl.ds(PLACE[k] * 64, 64)], region.at[k], region_send.at[k], region_recv.at[k],
            (me, above if k > 1 else below),
        )

    def late_edge(j, k):
        block = lax.rem(me + j, 16)
        return remote(
            mine.at[block, pl.ds(PLACE[k] * 64, 64)], region.at[k, block], strip_send.at[k // 3, j],
            strip_recv.at[k // 3, j], (me, above if k > 1 else below),
        )

    def seen_copy(i):
        return remote(seen_out.at[other(i)], measured.at[me], ob_send.at[i], ob_recv.at[i], (other(i), tile))

    def back(i, place):
        rows = pl.ds(place * 64, 64)
        return remote(
            sending.at[other(i), rows], returned.at[me, rows], back_send.at[place, i], back_recv.at[place, i],
            (other(i), tile),
        )

    for load in loads:
        load.wait()
    turn_in(x_ref, first, (0, 1, 6, 7))
    halo_out[1] = first[SPAN + 8:SPAN + 1032, :].astype(BF16)
    halo_out[0] = first[4 * SPAN + 8:4 * SPAN + 1032, :].astype(BF16)
    pl.semaphore_wait(barrier, 17)
    halo(0).start()
    halo(1).start()

    for load in small_loads:
        load.wait()
    sub = lax.broadcasted_iota(jnp.int32, (8, 128), 0)
    u = jnp.zeros((8, 128), F32)
    v = jnp.zeros((8, 128), F32)
    for level in range(4):
        column = jnp.broadcast_to(d_ref[level:level + 1, :], (128, 128)).T
        spread_d[pl.ds(level, 128, stride=8), :] = column
        spread_d[pl.ds(level + 4, 128, stride=8), :] = column
        here = lax.rem(sub, 4) == level
        u = jnp.where(here, 0.5 * u_ref[level], u)
        v = jnp.where(here, 0.5 * v_ref[level], v)
    turn_in(x_ref, first, (2, 3, 4, 5))
    wrap(first, (1, 2, 3, 4))
    upper = lax.broadcasted_iota(jnp.int32, (8, 8, 128), 1) < 4

    def coef(y0):
        return spread_d[pl.ds(pl.multiple_of(y0 * 8, 64), 64), :].reshape(8, 8, 128), u[None], v[None]

    def finish(k_list, block):
        y0 = block * 8
        for k, value in zip(k_list, stencil(second, k_list, 0, 5, y0, coef(y0), upper)):
            place = PLACE[k - 1] * 64
            mine[block, place:place + 64, :] = value.reshape(64, 128).astype(BF16)

    def inner(ahead):
        block = lax.rem(me + ahead, 16)
        y0 = block * 8
        for k, value in zip((1, 2, 3, 4), stencil(first, (1, 2, 3, 4), 1, 4, y0, coef(y0), upper)):
            second[pl.ds(pl.multiple_of(k * SPAN + (y0 + 1) * 8, 8), 64), :] = value.reshape(64, 128)

        @pl.when(block == 0)
        def _():
            for k in (2, 3):
                second[k * SPAN + 1032:k * SPAN + 1040, :] = second[k * SPAN + 8:k * SPAN + 16, :]

        @pl.when(block == 15)
        def _():
            for k in (2, 3):
                second[k * SPAN:k * SPAN + 8, :] = second[k * SPAN + 1024:k * SPAN + 1032, :]

    @pl.loop(0, 3)
    def _(ahead):
        inner(ahead)

    finish((2, 3), other(0))

    @pl.loop(1, 14)
    def _(i):
        inner(i + 2)
        finish((2, 3), other(i))
        state(i - 1).start()

    finish((2, 3), other(14))
    state(13).start()
    finish((2, 3), me)
    state(14).start()
    edge(1).start()
    edge(2).start()

    for i in range(16):
        cell = cell_ref[pl.ds(other(i), 1), :]
        place = cell % 256
        row, col = place // 16, place % 16
        level = cell // 256
        pair = row // 2
        own = (pair >= 2) & (pair <= 5)
        group = jnp.where(own, (pair - 2) // 2, jnp.where((pair == 0) | (pair == 7), 2, 3))
        second_of = jnp.where(own, pair % 2, jnp.where(pair >= 6, 1, 0))
        cells[0, i:i + 1, :] = (second_of * 128 + col * 8 + (row % 2) * 4 + level % 4).astype(F32)
        cells[1, i:i + 1, :] = (group + 4 * (level // 4)).astype(F32)
    index = jnp.concatenate([cells[0, :, 0:128].T, cells[0, :, 128:256].T], axis=0)
    choice = jnp.concatenate([cells[1, :, 0:128].T, cells[1, :, 128:256].T], axis=0)
    count = count_ref[0, 0]
    row_lane = lax.broadcasted_iota(jnp.int32, (1, 128), 1)
    root_rows, roots = [], []
    for part in range(2):
        root = jnp.sqrt(jnp.where(row_lane + 128 * part < count, weight_ref[part:part + 1, :], 0.0))
        root_rows.append(root)
        roots.append(jnp.broadcast_to(root, (128, 128)).T)

    for side in (0, 1):
        halo(side).wait()
        k = 5 * side
        first[k * SPAN + 8:k * SPAN + 1032, :] = halo_in[side].astype(F32)
    wrap(first, (0, 5))

    @pl.loop(0, 16)
    def _(step):
        y0 = step * 8
        d, u_c, v_c = coef(y0)
        for upper_k, lower_k, east_k, west_k, own in ((1, 0, 1, 0, 1), (5, 4, 5, 4, 4)):
            def rows(k, shift):
                return first[pl.ds(pl.multiple_of(k * SPAN + (y0 + 1 + shift) * 8, 8), 64), :].reshape(8, 8, 128)

            def mixed(shift):
                return jnp.where(upper, rows(upper_k, shift), rows(lower_k, shift))

            east = pltpu.roll(rows(east_k, 0), 4, 1)
            west = pltpu.roll(rows(west_k, 0), 4, 1)
            value = (
                mixed(0) * (1.0 - 4.0 * d) + east * (d - u_c) + west * (d + u_c)
                + mixed(1) * (d - v_c) + mixed(-1) * (d + v_c)
            )
            own_rows = pl.ds(pl.multiple_of(own * SPAN + (y0 + 1) * 8, 8), 64)
            kept = second[own_rows, :].reshape(8, 8, 128)
            kept = jnp.where(upper, value, kept) if own == 1 else jnp.where(upper, kept, value)
            second[own_rows, :] = kept.reshape(64, 128)
            side_k = 0 if own == 1 else 5
            second[pl.ds(pl.multiple_of(side_k * SPAN + (y0 + 1) * 8, 8), 64), :] = value.reshape(64, 128)

    wrap(second, (1, 4))
    finish((1, 4), me)
    finish((1, 4), other(0))
    late_edge(0, 0).start()
    late_edge(0, 3).start()

    @pl.loop(2, 16)
    def _(j):
        finish((1, 4), lax.rem(me + j, 16))
        late_edge(j - 1, 0).start()
        late_edge(j - 1, 3).start()
        late(j - 2, 0).start()

    late_edge(15, 0).start()
    late_edge(15, 3).start()
    late(14, 0).start()
    blocked[me] = mine[me]

    lane = lax.broadcasted_iota(jnp.int32, (256, 128), 1)
    lane_f = lane.astype(F32)
    left2 = lane < 64
    left = left2[0:128]

    lane_choice = jnp.where(left2, 0.0, 4.0)

    def picked(i, pairs):
        b = other(i)
        before, after = lax.rem(b + 15, 16), lax.rem(b + 1, 16)
        columns = []
        for group in pairs:
            pieces = []
            for kk in group:
                if 2 <= kk < 6:
                    place = PLACE[kk - 2] * 64
                    pieces.append(mine[before, place + 32:place + 64, :])
                    pieces.append(mine[b, place:place + 64, :])
                    pieces.append(mine[after, place:place + 32, :])
                else:
                    k = kk + 2 if kk < 2 else kk - 6
                    pieces.append(region[k, before, 32:64, :])
                    pieces.append(region[k, b, :, :])
                    pieces.append(region[k, after, 0:32, :])
            columns.append(jnp.concatenate(pieces, axis=0))
        return nn(hot[i], jnp.concatenate(columns, axis=1))

    for i in range(16):
        here = jnp.broadcast_to(index[:, i:i + 1], (256, 128))
        hot[i, :, 0:128] = jnp.where(here == lane_f, 1.0, 0.0).astype(BF16)
        hot[i, :, 128:256] = jnp.where(here == lane_f + 128.0, 1.0, 0.0).astype(BF16)
        values = picked(i, ((2, 3), (4, 5)))
        wanted = choice[:, i:i + 1] - lane_choice
        seen[i] = jnp.where(wanted == 0.0, values[:, 0:128], jnp.where(wanted == 1.0, values[:, 128:256], 0.0))
    edge(1).wait()
    edge(2).wait()
    for i in range(16):
        for j in (0, 1, 2) if i == 0 else (i + 2,):
            if j < 16:
                late_edge(j, 0).wait()
                late_edge(j, 3).wait()
        values = picked(i, ((0, 7), (1, 6)))
        wanted = choice[:, i:i + 1] - lane_choice
        values = jnp.where(wanted == 2.0, values[:, 0:128], jnp.where(wanted == 3.0, values[:, 128:256], seen[i]))
        values = values + pltpu.roll(values, 64, 1)
        packed = jnp.where(left, values[0:128], values[128:256]).astype(BF16)
        if i < 15:
            seen_out[other(i)] = packed
        else:
            measured[me] = packed
        if i > 0:
            seen_copy(i - 1).start()

    @pl.loop(0, 15)
    def _(i):
        late(i, 1).start()

    def centred(start, count):
        rows = slice(start, start + count)
        left_rows = left2[rows]
        total = blocked[0, rows, :].astype(F32)
        for g in range(1, 16):
            total = total + blocked[g, rows, :].astype(F32)
        centre0 = jnp.sum(jnp.where(left_rows, total, 0.0), axis=1, keepdims=True) * (1.0 / MEMBERS)
        centre1 = jnp.sum(jnp.where(left_rows, 0.0, total), axis=1, keepdims=True) * (1.0 / MEMBERS)
        centre = jnp.where(left_rows, centre0, centre1)
        target = (start // 128) * 256 + start % 128
        for q in range(8):
            even = blocked[other(2 * q), rows, :].astype(F32) - centre
            odd = blocked[other(2 * q + 1), rows, :].astype(F32) - centre
            lanes = slice(q * 128, (q + 1) * 128)
            dev[target:target + count, lanes] = jnp.where(left_rows, even, pltpu.roll(odd, 64, 1)).astype(BF16)
            dev[target + 128:target + 128 + count, lanes] = jnp.where(
                left_rows, pltpu.roll(even, 64, 1), odd
            ).astype(BF16)
        return centre0, centre1

    @pl.loop(0, 15)
    def _(i):
        state(i).wait()

    centre_a = centred(0, 128)

    @pl.loop(0, 15)
    def _(i):
        late(i, 0).wait()

    centre_b = centred(128, 64)

    @pl.loop(0, 15)
    def _(i):
        seen_copy(i).wait()

    total = measured[0].astype(F32)
    for g in range(1, 16):
        total = total + measured[g].astype(F32)
    mean0 = jnp.sum(jnp.where(left, total, 0.0), axis=1, keepdims=True) * (1.0 / MEMBERS)
    mean1 = jnp.sum(jnp.where(left, 0.0, total), axis=1, keepdims=True) * (1.0 / MEMBERS)
    misfit = jnp.concatenate(
        [
            root_rows[part] * (value_ref[part:part + 1, :] - jnp.broadcast_to(mean, (128, 128)).T[0:1])
            for part, mean in enumerate((mean0, mean1))
        ],
        axis=1,
    )
    mean = jnp.where(left, mean0, mean1)
    root = jnp.where(left, roots[0], roots[1])
    for q in range(8):
        even = (measured[other(2 * q)].astype(F32) - mean) * root
        odd = (measured[other(2 * q + 1)].astype(F32) - mean) * root
        lanes = slice(q * 128, (q + 1) * 128)
        basis[0:128, lanes] = jnp.where(left, even, pltpu.roll(odd, 64, 1)).astype(BF16)
        basis[128:256, lanes] = jnp.where(left, pltpu.roll(even, 64, 1), odd).astype(BF16)
    small = nt(basis[...], basis[...])
    eye = lax.broadcasted_iota(jnp.int32, (256, 256), 0) == lax.broadcasted_iota(jnp.int32, (256, 256), 1)
    trace = jnp.sum(jnp.where(eye, small, 0.0), axis=(0, 1), keepdims=True)
    s = (MEMBERS - 1.0) + trace * (1.0 / MEMBERS)
    inv_s = 1.0 / s
    inv_root_s = lax.rsqrt(s)
    a = (MEMBERS - 1.0) * inv_s
    p = 1.5 - 0.5 * a
    r0 = 1.5 * p - 0.5 * a * p * p * p
    r1 = -0.75 - 0.5 * p * p * p + 0.75 * a * p * p
    r2 = 0.5 * (1.5 * p * p - 0.75 * a * p)
    r3 = (1.0 / 6.0) * (0.375 * a - 2.25 * p)
    r4 = 1.5 / 24.0
    spread = jnp.sqrt(jnp.full((1, 1), MEMBERS - 1.0, F32))
    keep = r0 * spread * inv_root_s
    g1 = small * inv_s
    g1_s = split(g1)
    g2 = nn3(g1_s, g1_s)
    g2_s = split(g2)
    q = jnp.where(eye, r1, 0.0) + r2 * g1 + r3 * g2 + r4 * nn3(g2_s, g1_s)
    mix_s = split(q * (spread * inv_s * inv_root_s))

    def through(row):
        column = jnp.sum(q * row, axis=1, keepdims=True)
        return (r0 * row + jnp.sum(g1 * column, axis=0, keepdims=True)) * inv_root_s

    gain = through(through(misfit))

    def answer(part, centre):
        here = slice(part * 256, part * 256 + 256)
        rows = slice(part * 128, part * 128 + 128)
        cross = nt(dev[here, :], basis[...])
        update = nn3(split(cross), mix_s).astype(BF16)
        offset = centre + jnp.sum(cross * gain, axis=1, keepdims=True)
        for double in range(4):
            lanes = slice(double * 256, double * 256 + 256)
            both = offset + keep * dev[here, lanes].astype(F32) + nn(update, basis[:, lanes])
            for q in (2 * double, 2 * double + 1):
                value = both[:, 0:128] if q % 2 == 0 else both[:, 128:256]
                var0, var1 = value[0:128], value[128:256]
                sending[other(2 * q), rows, :] = jnp.where(left, var0, pltpu.roll(var1, 64, 1)).astype(BF16)
                odd = jnp.where(left, pltpu.roll(var0, 64, 1), var1).astype(BF16)
                if q < 7:
                    sending[other(2 * q + 1), rows, :] = odd
                else:
                    returned[me, rows, :] = odd
                if q > 0:
                    back(2 * q - 2, 2 * part).start()
                    back(2 * q - 1, 2 * part).start()
        back(14, 2 * part).start()

        @pl.loop(0, 15)
        def _(i):
            back(i, 2 * part + 1).start()

    answer(0, jnp.concatenate(centre_a, axis=0))

    @pl.loop(0, 15)
    def _(i):
        late(i, 1).wait()

    centre_c = centred(192, 64)
    answer(1, jnp.concatenate([centre_b[0], centre_c[0], centre_b[1], centre_c[1]], axis=0))

    for place in range(4):
        @pl.loop(0, 15)
        def _(i):
            back(i, place).wait()

        turn_out(returned, first, second, place)
    out_ref[...] = second[0:4096, :].astype(BF16)


def call_whole(x, d, u, v, cell, weight, value, count):
    dma = pltpu.SemaphoreType.DMA
    return pl.pallas_call(
        whole,
        out_shape=jax.ShapeDtypeStruct((4096, 128), BF16),
        in_specs=[ANY] * 7 + [pl.BlockSpec(memory_space=pltpu.SMEM)],
        out_specs=VMEM,
        scratch_shapes=[
            pltpu.VMEM((4, 128), F32),
            pltpu.SMEM((4,), F32),
            pltpu.SMEM((4,), F32),
            pltpu.VMEM((16, 256), jnp.int32),
            pltpu.VMEM((2, 128), F32),
            pltpu.VMEM((2, 128), F32),
            dma((6,)),
            pltpu.VMEM((4096, 128), F32),
            pltpu.VMEM((6 * SPAN, 128), F32),
            pltpu.VMEM((6 * SPAN, 128), F32),
            pltpu.VMEM((1024, 128), F32),
            pltpu.VMEM((2, 128, 256), F32),
            pltpu.VMEM((16, 256, 256), BF16),
            pltpu.VMEM((2, 1024, 128), BF16),
            pltpu.VMEM((2, 1024, 128), BF16),
            pltpu.VMEM((16, 256, 128), BF16),
            pltpu.VMEM((16, 256, 128), BF16),
            pltpu.VMEM((4, 16, 64, 128), BF16),
            pltpu.VMEM((16, 256, 128), F32),
            pltpu.VMEM((16, 128, 128), BF16),
            pltpu.VMEM((16, 128, 128), BF16),
            pltpu.VMEM((512, 1024), BF16),
            pltpu.VMEM((256, 1024), BF16),
            pltpu.VMEM((16, 256, 128), BF16),
            pltpu.VMEM((16, 256, 128), BF16),
            dma((4,)), dma((2,)), dma((2,)), dma((15,)), dma((15,)), dma((2, 15)), dma((2, 15)), dma((4,)), dma((4,)),
            dma((2, 16)), dma((2, 16)), dma((15,)), dma((15,)), dma((4, 15)), dma((4, 15)),
        ],
        compiler_params=pltpu.CompilerParams(
            vmem_limit_bytes=48000000, collective_id=0, has_side_effects=True
        ),
        name="whole",
    )(x, d, u, v, cell, weight, value, count)


def hbm(x):
    return pltpu.with_memory_space_constraint(x, pltpu.MemorySpace.HBM)


def on_device(
    starting_realizations,
    diffusivity,
    eastward_velocity,
    northward_velocity,
    obs_cell,
    obs_count,
    obs_value,
    obs_weight,
):
    analysis = call_whole(
        hbm(starting_realizations.reshape(4096, 128)), hbm(diffusivity), hbm(eastward_velocity), hbm(northward_velocity),
        hbm(obs_cell[0]), hbm(obs_weight.reshape(2, 128)), hbm(obs_value.reshape(2, 128)), obs_count,
    )
    return analysis.reshape(64, 2, 4, 8, 128)


def solution(mesh):
    return jax.shard_map(
        on_device,
        mesh=mesh,
        in_specs=(
            P("grp", None, None, "tile", None),
            P(),
            P(),
            P(),
            P("tile", None, None),
            P("tile", "grp"),
            P("tile", "grp", None),
            P("tile", "grp", None),
        ),
        out_specs=P("grp", None, None, "tile", None),
        check_vma=False,
    )
```

```python
import jax
import jax.numpy as jnp
from jax import lax
from jax.experimental import pallas as pl
from jax.experimental.pallas import tpu as pltpu
from jax.sharding import PartitionSpec as P


F32 = jnp.float32
BF16 = jnp.bfloat16
VMEM = pl.BlockSpec(memory_space=pltpu.VMEM)
MEMBERS = 1024.0
MESH = pl.DeviceIdType.MESH
ANY = pl.BlockSpec(memory_space=pl.ANY)
PLACE = (2, 0, 1, 3)
PAIR = (1, 2, 0, 3)
FAR = (10, 6, 9, 14, 11, 2, 8, 5, 15, 7, 13, 1, 4, 3, 12, 0)
SPAN = 130 * 8


def nt(a, b):
    return lax.dot_general(a, b, (((1,), (1,)), ((), ())), preferred_element_type=F32)


def nn(a, b):
    return lax.dot_general(a, b, (((1,), (0,)), ((), ())), preferred_element_type=F32)


def split(a):
    top = a.astype(BF16)
    return top, (a - top.astype(F32)).astype(BF16)


def nn3(a, b):
    (a0, a1), (b0, b1) = a, b
    return nn(jnp.concatenate([a0, a0, a1], axis=1), jnp.concatenate([b0, b1, b0], axis=0))


def stencil(ref, k_list, low, high, y0, coef, upper):
    d, u, v = coef
    east_c, west_c, north_c, south_c = d - u, d + u, d - v, d + v
    mid_c = 1.0 - 4.0 * d

    def rows(k, shift):
        return ref[pl.ds(pl.multiple_of(k * SPAN + (y0 + 1 + shift) * 8, 8), 64), :].reshape(8, 8, 128)

    rolled = {}

    def roll(k):
        if k not in rolled:
            rolled[k] = pltpu.roll(rows(k, 0), 4, 1)
        return rolled[k]

    outs = []
    for k in k_list:
        east = jnp.where(upper, roll(k), roll(k + 1)) if k < high else roll(k)
        west = jnp.where(upper, roll(k - 1), roll(k)) if k > low else roll(k)
        outs.append(
            rows(k, 0) * mid_c + east * east_c + west * west_c + rows(k, 1) * north_c + rows(k, -1) * south_c
        )
    return outs


def wrap(ref, k_list):
    for k in k_list:
        ref[k * SPAN:k * SPAN + 8, :] = ref[k * SPAN + 1024:k * SPAN + 1032, :]
        ref[k * SPAN + 1032:k * SPAN + 1040, :] = ref[k * SPAN + 8:k * SPAN + 16, :]


def turn_in(x_ref, field, rows):
    for row in rows:
        for level in range(4):
            start = level * 8 + row
            plane = jnp.concatenate(
                [x_ref[pl.ds(start, 64, stride=64), :], x_ref[pl.ds(start + 32, 64, stride=64), :]], axis=0
            )
            start = (row // 2 + 1) * SPAN + 8 + (row % 2) * 4 + level
            field[pl.ds(start, 128, stride=8), :] = plane.T


def turn_out(returned, field, stage, place):
    k = PAIR[place]
    for b in range(16):
        field[k * 1024 + b * 64:k * 1024 + b * 64 + 64, :] = returned[b, place * 64:place * 64 + 64, :].astype(F32)
    for row in (2 * k, 2 * k + 1):
        for level in range(4):
            start = level * 8 + row
            plane = field[pl.ds(k * 1024 + (row % 2) * 4 + level, 128, stride=8), :].T
            stage[pl.ds(start, 64, stride=64), :] = plane[0:64]
            stage[pl.ds(start + 32, 64, stride=64), :] = plane[64:128]


def whole(
    x_hbm, d_hbm, u_hbm, v_hbm, cell_hbm, weight_hbm, value_hbm, count_ref, out_ref,
    d_ref, u_ref, v_ref, cell_ref, weight_ref, value_ref, small_sem, x_ref, first, second, spread_d, cells, hot, halo_out, halo_in, mine, blocked, region, seen, seen_out, measured,
    dev, basis, sending, returned,
    load_sem, halo_send, halo_recv, state_send, state_recv, late_send, late_recv, region_send, region_recv,
    strip_send, strip_recv, ob_send, ob_recv, back_send, back_recv,
):
    me = lax.axis_index("grp")
    tile = lax.axis_index("tile")
    tiles = lax.axis_size("tile")
    below, above = lax.rem(tile + tiles - 1, tiles), lax.rem(tile + 1, tiles)

    def other(i):
        return lax.rem(me + 1 + i, 16)

    small_loads = []
    for source, target in (
        (d_hbm, d_ref), (u_hbm, u_ref), (v_hbm, v_ref), (cell_hbm, cell_ref), (weight_hbm, weight_ref),
        (value_hbm, value_ref),
    ):
        small_loads.append(pltpu.make_async_copy(source, target, small_sem.at[len(small_loads)]))
        small_loads[-1].start()
    loads = []
    for piece in range(4):
        rows = pl.ds(piece * 1024, 1024)
        loads.append(pltpu.make_async_copy(x_hbm.at[rows], x_ref.at[rows], load_sem.at[piece]))
        loads[-1].start()
    barrier = pltpu.get_barrier_semaphore()

    @pl.loop(0, 15)
    def _(i):
        pl.semaphore_signal(barrier, inc=1, device_id=(other(i), tile), device_id_type=MESH)

    pl.semaphore_signal(barrier, inc=1, device_id=(me, below), device_id_type=MESH)
    pl.semaphore_signal(barrier, inc=1, device_id=(me, above), device_id_type=MESH)

    def remote(source, target, send, recv, device):
        return pltpu.make_async_remote_copy(
            src_ref=source, dst_ref=target, send_sem=send, recv_sem=recv, device_id=device, device_id_type=MESH
        )

    def halo(side):
        return remote(
            halo_out.at[side], halo_in.at[side], halo_send.at[side], halo_recv.at[side],
            (me, above if side == 0 else below),
        )

    def state(i):
        rows = pl.ds(0, 128)
        return remote(
            mine.at[other(i), rows], blocked.at[me, rows], state_send.at[i], state_recv.at[i], (other(i), tile)
        )

    def late(i, part):
        rows = pl.ds(128 + 64 * part, 64)
        return remote(
            mine.at[other(i), rows], blocked.at[me, rows], late_send.at[part, i], late_recv.at[part, i],
            (other(i), tile),
        )

    def edge(k):
        return remote(
            mine.at[:, pl.ds(PLACE[k] * 64, 64)], region.at[k], region_send.at[k], region_recv.at[k],
            (me, above if k > 1 else below),
        )

    def late_edge(j, k):
        block = lax.rem(me + j, 16)
        return remote(
            mine.at[block, pl.ds(PLACE[k] * 64, 64)], region.at[k, block], strip_send.at[k // 3, j],
            strip_recv.at[k // 3, j], (me, above if k > 1 else below),
        )

    def seen_copy(i):
        return remote(seen_out.at[other(i)], measured.at[me], ob_send.at[i], ob_recv.at[i], (other(i), tile))

    def toward(i):
        return lax.rem(me // 4 + FAR[i] // 4, 4) * 4 + lax.rem(me + FAR[i] % 4, 4)

    def back(i, part):
        rows = pl.ds(part * 128, 128)
        return remote(
            sending.at[toward(i), rows], returned.at[me, rows], back_send.at[part, i], back_recv.at[part, i],
            (toward(i), tile),
        )

    for load in small_loads:
        load.wait()
    sub = lax.broadcasted_iota(jnp.int32, (8, 128), 0)
    u = jnp.zeros((8, 128), F32)
    v = jnp.zeros((8, 128), F32)
    for level in range(4):
        column = jnp.broadcast_to(d_ref[level:level + 1, :], (128, 128)).T
        spread_d[pl.ds(level, 128, stride=8), :] = column
        spread_d[pl.ds(level + 4, 128, stride=8), :] = column
        here = lax.rem(sub, 4) == level
        u = jnp.where(here, 0.5 * u_ref[level], u)
        v = jnp.where(here, 0.5 * v_ref[level], v)

    for load in loads:
        load.wait()
    turn_in(x_ref, first, (0, 1, 6, 7))
    halo_out[1] = first[SPAN + 8:SPAN + 1032, :].astype(BF16)
    halo_out[0] = first[4 * SPAN + 8:4 * SPAN + 1032, :].astype(BF16)
    pl.semaphore_wait(barrier, 17)
    halo(0).start()
    halo(1).start()

    turn_in(x_ref, first, (2, 3, 4, 5))
    wrap(first, (1, 2, 3, 4))
    upper = lax.broadcasted_iota(jnp.int32, (8, 8, 128), 1) < 4

    def coef(y0):
        return spread_d[pl.ds(pl.multiple_of(y0 * 8, 64), 64), :].reshape(8, 8, 128), u[None], v[None]

    def finish(k_list, block):
        y0 = block * 8
        for k, value in zip(k_list, stencil(second, k_list, 0, 5, y0, coef(y0), upper)):
            place = PLACE[k - 1] * 64
            mine[block, place:place + 64, :] = value.reshape(64, 128).astype(BF16)

    def inner(ahead):
        block = lax.rem(me + ahead, 16)
        y0 = block * 8
        for k, value in zip((1, 2, 3, 4), stencil(first, (1, 2, 3, 4), 1, 4, y0, coef(y0), upper)):
            second[pl.ds(pl.multiple_of(k * SPAN + (y0 + 1) * 8, 8), 64), :] = value.reshape(64, 128)

        @pl.when(block == 0)
        def _():
            for k in (2, 3):
                second[k * SPAN + 1032:k * SPAN + 1040, :] = second[k * SPAN + 8:k * SPAN + 16, :]

        @pl.when(block == 15)
        def _():
            for k in (2, 3):
                second[k * SPAN:k * SPAN + 8, :] = second[k * SPAN + 1024:k * SPAN + 1032, :]

    @pl.loop(0, 3)
    def _(ahead):
        inner(ahead)

    finish((2, 3), other(0))

    @pl.loop(1, 14)
    def _(i):
        inner(i + 2)
        finish((2, 3), other(i))
        state(i - 1).start()

    finish((2, 3), other(14))
    state(13).start()
    finish((2, 3), me)
    state(14).start()
    edge(1).start()
    edge(2).start()

    for i in range(16):
        cell = cell_ref[pl.ds(other(i), 1), :]
        place = cell % 256
        row, col = place // 16, place % 16
        level = cell // 256
        pair = row // 2
        own = (pair >= 2) & (pair <= 5)
        group = jnp.where(own, (pair - 2) // 2, jnp.where((pair == 0) | (pair == 7), 2, 3))
        second_of = jnp.where(own, pair % 2, jnp.where(pair >= 6, 1, 0))
        cells[0, i:i + 1, :] = (second_of * 128 + col * 8 + (row % 2) * 4 + level % 4).astype(F32)
        cells[1, i:i + 1, :] = (group + 4 * (level // 4)).astype(F32)
    index = jnp.concatenate([cells[0, :, 0:128].T, cells[0, :, 128:256].T], axis=0)
    choice = jnp.concatenate([cells[1, :, 0:128].T, cells[1, :, 128:256].T], axis=0)
    count = count_ref[0, 0]
    row_lane = lax.broadcasted_iota(jnp.int32, (1, 128), 1)
    root_rows, roots = [], []
    for part in range(2):
        root = jnp.sqrt(jnp.where(row_lane + 128 * part < count, weight_ref[part:part + 1, :], 0.0))
        root_rows.append(root)
        roots.append(jnp.broadcast_to(root, (128, 128)).T)

    for side in (0, 1):
        halo(side).wait()
        k = 5 * side
        first[k * SPAN + 8:k * SPAN + 1032, :] = halo_in[side].astype(F32)
    wrap(first, (0, 5))

    @pl.loop(0, 16)
    def _(step):
        y0 = step * 8
        d, u_c, v_c = coef(y0)
        for upper_k, lower_k, east_k, west_k, own in ((1, 0, 1, 0, 1), (5, 4, 5, 4, 4)):
            def rows(k, shift):
                return first[pl.ds(pl.multiple_of(k * SPAN + (y0 + 1 + shift) * 8, 8), 64), :].reshape(8, 8, 128)

            def mixed(shift):
                return jnp.where(upper, rows(upper_k, shift), rows(lower_k, shift))

            east = pltpu.roll(rows(east_k, 0), 4, 1)
            west = pltpu.roll(rows(west_k, 0), 4, 1)
            value = (
                mixed(0) * (1.0 - 4.0 * d) + east * (d - u_c) + west * (d + u_c)
                + mixed(1) * (d - v_c) + mixed(-1) * (d + v_c)
            )
            own_rows = pl.ds(pl.multiple_of(own * SPAN + (y0 + 1) * 8, 8), 64)
            kept = second[own_rows, :].reshape(8, 8, 128)
            kept = jnp.where(upper, value, kept) if own == 1 else jnp.where(upper, kept, value)
            second[own_rows, :] = kept.reshape(64, 128)
            side_k = 0 if own == 1 else 5
            second[pl.ds(pl.multiple_of(side_k * SPAN + (y0 + 1) * 8, 8), 64), :] = value.reshape(64, 128)

    wrap(second, (1, 4))
    finish((1, 4), me)
    finish((1, 4), other(0))
    late_edge(0, 0).start()
    late_edge(0, 3).start()

    @pl.loop(2, 16)
    def _(j):
        finish((1, 4), lax.rem(me + j, 16))
        late_edge(j - 1, 0).start()
        late_edge(j - 1, 3).start()
        late(j - 2, 0).start()

    late_edge(15, 0).start()
    late_edge(15, 3).start()
    late(14, 0).start()
    blocked[me] = mine[me]

    lane = lax.broadcasted_iota(jnp.int32, (256, 128), 1)
    lane_f = lane.astype(F32)
    left2 = lane < 64
    left = left2[0:128]

    lane_choice = jnp.where(left2, 0.0, 4.0)

    def picked(i, pairs):
        b = other(i)
        before, after = lax.rem(b + 15, 16), lax.rem(b + 1, 16)
        columns = []
        for group in pairs:
            pieces = []
            for kk in group:
                if 2 <= kk < 6:
                    place = PLACE[kk - 2] * 64
                    pieces.append(mine[before, place + 32:place + 64, :])
                    pieces.append(mine[b, place:place + 64, :])
                    pieces.append(mine[after, place:place + 32, :])
                else:
                    k = kk + 2 if kk < 2 else kk - 6
                    pieces.append(region[k, before, 32:64, :])
                    pieces.append(region[k, b, :, :])
                    pieces.append(region[k, after, 0:32, :])
            columns.append(jnp.concatenate(pieces, axis=0))
        return nn(hot[i], jnp.concatenate(columns, axis=1))

    for i in range(16):
        here = jnp.broadcast_to(index[:, i:i + 1], (256, 128))
        hot[i, :, 0:128] = jnp.where(here == lane_f, 1.0, 0.0).astype(BF16)
        hot[i, :, 128:256] = jnp.where(here == lane_f + 128.0, 1.0, 0.0).astype(BF16)
        values = picked(i, ((2, 3), (4, 5)))
        wanted = choice[:, i:i + 1] - lane_choice
        seen[i] = jnp.where(wanted == 0.0, values[:, 0:128], jnp.where(wanted == 1.0, values[:, 128:256], 0.0))
    edge(1).wait()
    edge(2).wait()
    for i in range(16):
        for j in (0, 1, 2) if i == 0 else (i + 2,):
            if j < 16:
                late_edge(j, 0).wait()
                late_edge(j, 3).wait()
        values = picked(i, ((0, 7), (1, 6)))
        wanted = choice[:, i:i + 1] - lane_choice
        values = jnp.where(wanted == 2.0, values[:, 0:128], jnp.where(wanted == 3.0, values[:, 128:256], seen[i]))
        values = values + pltpu.roll(values, 64, 1)
        packed = jnp.where(left, values[0:128], values[128:256]).astype(BF16)
        if i < 15:
            seen_out[other(i)] = packed
        else:
            measured[me] = packed
        if i > 0:
            seen_copy(i - 1).start()

    @pl.loop(0, 15)
    def _(i):
        late(i, 1).start()

    def centred(start, count):
        rows = slice(start, start + count)
        left_rows = left2[rows]
        total = blocked[0, rows, :].astype(F32)
        for g in range(1, 16):
            total = total + blocked[g, rows, :].astype(F32)
        centre0 = jnp.sum(jnp.where(left_rows, total, 0.0), axis=1, keepdims=True) * (1.0 / MEMBERS)
        centre1 = jnp.sum(jnp.where(left_rows, 0.0, total), axis=1, keepdims=True) * (1.0 / MEMBERS)
        centre = jnp.where(left_rows, centre0, centre1)
        target = (start // 128) * 256 + start % 128
        for q in range(8):
            even = blocked[toward(2 * q), rows, :].astype(F32) - centre
            odd = blocked[toward(2 * q + 1), rows, :].astype(F32) - centre
            lanes = slice(q * 128, (q + 1) * 128)
            dev[target:target + count, lanes] = jnp.where(left_rows, even, pltpu.roll(odd, 64, 1)).astype(BF16)
            dev[target + 128:target + 128 + count, lanes] = jnp.where(
                left_rows, pltpu.roll(even, 64, 1), odd
            ).astype(BF16)
        return centre0, centre1

    @pl.loop(0, 15)
    def _(i):
        state(i).wait()

    centre_a = centred(0, 128)

    @pl.loop(0, 15)
    def _(i):
        late(i, 0).wait()

    centre_b = centred(128, 64)

    @pl.loop(0, 15)
    def _(i):
        seen_copy(i).wait()

    total = measured[0].astype(F32)
    for g in range(1, 16):
        total = total + measured[g].astype(F32)
    mean0 = jnp.sum(jnp.where(left, total, 0.0), axis=1, keepdims=True) * (1.0 / MEMBERS)
    mean1 = jnp.sum(jnp.where(left, 0.0, total), axis=1, keepdims=True) * (1.0 / MEMBERS)
    misfit = jnp.concatenate(
        [
            root_rows[part] * (value_ref[part:part + 1, :] - jnp.broadcast_to(mean, (128, 128)).T[0:1])
            for part, mean in enumerate((mean0, mean1))
        ],
        axis=1,
    )
    mean = jnp.where(left, mean0, mean1)
    root = jnp.where(left, roots[0], roots[1])
    for q in range(8):
        even = (measured[toward(2 * q)].astype(F32) - mean) * root
        odd = (measured[toward(2 * q + 1)].astype(F32) - mean) * root
        lanes = slice(q * 128, (q + 1) * 128)
        basis[0:128, lanes] = jnp.where(left, even, pltpu.roll(odd, 64, 1)).astype(BF16)
        basis[128:256, lanes] = jnp.where(left, pltpu.roll(even, 64, 1), odd).astype(BF16)
    small = nt(basis[...], basis[...])
    eye = lax.broadcasted_iota(jnp.int32, (256, 256), 0) == lax.broadcasted_iota(jnp.int32, (256, 256), 1)
    trace = jnp.sum(jnp.where(eye, small, 0.0), axis=(0, 1), keepdims=True)
    s = (MEMBERS - 1.0) + trace * (1.0 / MEMBERS)
    inv_s = 1.0 / s
    inv_root_s = lax.rsqrt(s)
    a = (MEMBERS - 1.0) * inv_s
    p = 1.5 - 0.5 * a
    r0 = 1.5 * p - 0.5 * a * p * p * p
    r1 = -0.75 - 0.5 * p * p * p + 0.75 * a * p * p
    r2 = 0.5 * (1.5 * p * p - 0.75 * a * p)
    r3 = (1.0 / 6.0) * (0.375 * a - 2.25 * p)
    r4 = 1.5 / 24.0
    spread = jnp.sqrt(jnp.full((1, 1), MEMBERS - 1.0, F32))
    keep = r0 * spread * inv_root_s
    g1 = small * inv_s
    g1_s = split(g1)
    g2 = nn3(g1_s, g1_s)
    g2_s = split(g2)
    q = jnp.where(eye, r1, 0.0) + r2 * g1 + r3 * g2 + r4 * nn3(g2_s, g1_s)
    mix_s = split(q * (spread * inv_s * inv_root_s))

    def through(row):
        column = jnp.sum(q * row, axis=1, keepdims=True)
        return (r0 * row + jnp.sum(g1 * column, axis=0, keepdims=True)) * inv_root_s

    gain = through(through(misfit))

    def answer(part, centre):
        here = slice(part * 256, part * 256 + 256)
        rows = slice(part * 128, part * 128 + 128)
        cross = nt(dev[here, :], basis[...])
        update = nn3(split(cross), mix_s).astype(BF16)
        offset = centre + jnp.sum(cross * gain, axis=1, keepdims=True)
        for double in range(4):
            lanes = slice(double * 256, double * 256 + 256)
            both = offset + keep * dev[here, lanes].astype(F32) + nn(update, basis[:, lanes])
            for q in (2 * double, 2 * double + 1):
                value = both[:, 0:128] if q % 2 == 0 else both[:, 128:256]
                var0, var1 = value[0:128], value[128:256]
                sending[toward(2 * q), rows, :] = jnp.where(left, var0, pltpu.roll(var1, 64, 1)).astype(BF16)
                odd = jnp.where(left, pltpu.roll(var0, 64, 1), var1).astype(BF16)
                if q < 7:
                    sending[toward(2 * q + 1), rows, :] = odd
                else:
                    returned[me, rows, :] = odd
                if q > 0:
                    back(2 * q - 2, part).start()
                    back(2 * q - 1, part).start()
        back(14, part).start()

    answer(0, jnp.concatenate(centre_a, axis=0))

    @pl.loop(0, 15)
    def _(i):
        late(i, 1).wait()

    centre_c = centred(192, 64)
    answer(1, jnp.concatenate([centre_b[0], centre_c[0], centre_b[1], centre_c[1]], axis=0))

    for part in range(2):
        for i in range(15):
            back(i, part).wait()

        turn_out(returned, first, second, 2 * part)
        turn_out(returned, first, second, 2 * part + 1)
    out_ref[...] = second[0:4096, :].astype(BF16)


def call_whole(x, d, u, v, cell, weight, value, count):
    dma = pltpu.SemaphoreType.DMA
    return pl.pallas_call(
        whole,
        out_shape=jax.ShapeDtypeStruct((4096, 128), BF16),
        in_specs=[ANY] * 7 + [pl.BlockSpec(memory_space=pltpu.SMEM)],
        out_specs=VMEM,
        scratch_shapes=[
            pltpu.VMEM((4, 128), F32),
            pltpu.SMEM((4,), F32),
            pltpu.SMEM((4,), F32),
            pltpu.VMEM((16, 256), jnp.int32),
            pltpu.VMEM((2, 128), F32),
            pltpu.VMEM((2, 128), F32),
            dma((6,)),
            pltpu.VMEM((4096, 128), F32),
            pltpu.VMEM((6 * SPAN, 128), F32),
            pltpu.VMEM((6 * SPAN, 128), F32),
            pltpu.VMEM((1024, 128), F32),
            pltpu.VMEM((2, 128, 256), F32),
            pltpu.VMEM((16, 256, 256), BF16),
            pltpu.VMEM((2, 1024, 128), BF16),
            pltpu.VMEM((2, 1024, 128), BF16),
            pltpu.VMEM((16, 256, 128), BF16),
            pltpu.VMEM((16, 256, 128), BF16),
            pltpu.VMEM((4, 16, 64, 128), BF16),
            pltpu.VMEM((16, 256, 128), F32),
            pltpu.VMEM((16, 128, 128), BF16),
            pltpu.VMEM((16, 128, 128), BF16),
            pltpu.VMEM((512, 1024), BF16),
            pltpu.VMEM((256, 1024), BF16),
            pltpu.VMEM((16, 256, 128), BF16),
            pltpu.VMEM((16, 256, 128), BF16),
            dma((4,)), dma((2,)), dma((2,)), dma((15,)), dma((15,)), dma((2, 15)), dma((2, 15)), dma((4,)), dma((4,)),
            dma((2, 16)), dma((2, 16)), dma((15,)), dma((15,)), dma((2, 15)), dma((2, 15)),
        ],
        compiler_params=pltpu.CompilerParams(
            vmem_limit_bytes=48000000, collective_id=0, has_side_effects=True
        ),
        name="whole",
    )(x, d, u, v, cell, weight, value, count)


def hbm(x):
    return pltpu.with_memory_space_constraint(x, pltpu.MemorySpace.HBM)


def on_device(
    starting_realizations,
    diffusivity,
    eastward_velocity,
    northward_velocity,
    obs_cell,
    obs_count,
    obs_value,
    obs_weight,
):
    analysis = call_whole(
        hbm(starting_realizations.reshape(4096, 128)), hbm(diffusivity), hbm(eastward_velocity), hbm(northward_velocity),
        hbm(obs_cell[0]), hbm(obs_weight.reshape(2, 128)), hbm(obs_value.reshape(2, 128)), obs_count,
    )
    return analysis.reshape(64, 2, 4, 8, 128)


def solution(mesh):
    return jax.shard_map(
        on_device,
        mesh=mesh,
        in_specs=(
            P("grp", None, None, "tile", None),
            P(),
            P(),
            P(),
            P("tile", None, None),
            P("tile", "grp"),
            P("tile", "grp", None),
            P("tile", "grp", None),
        ),
        out_specs=P("grp", None, None, "tile", None),
        check_vma=False,
    )
```
